128 devices in a mesh: rows: 128 (over z, x, y, core).
Axes of the slice: x: 4, y: 4, z: 4, core: 2. Of those that a mesh axis runs over, the one named last changes fastest.
Arguments:
- covariates: float32 [262144, 128], P('rows'), may hold values from -24 to 24
- outcome: float32 [262144], P('rows'), may hold values from 0 to 3
- predictor: float32 [262144], P('rows'), may hold values from -1.5 to 1.5
- firm_id: int32 [262144], P('rows'), may hold values from 0 to 127
- dy_id: int32 [262144], P('rows'), may hold values from 0 to 2047
- pd_owner: int32 [262144, 1], P('rows'), may hold values from 0 to 127; in each aligned block of 2048 rows (0 to 2047, 2048 to 4095, ...) at most 32 rows name the same one
- pd_local: int32 [262144], P('rows'), may hold values from 0 to 15
Outputs:
- x_tilde: float32 [262144, 128], P('rows')
- z_tilde: float32 [262144], P('rows')
- gram: float32 [128, 128], P('rows')
- rhs: float32 [128], P('rows')
The draws below stay inside these ranges and needn't reach their ends.
Inputs may be any that keep to these rules, and one draw needn't show every extreme that they name: `pd_owner`: among the rows of one device no owner is named more than 32 times, a bound that some block reaches.
All inputs are finite; a program needn't handle non-finite values.
Results may differ from the reference program's by a relative error of at most 0.0003.
Values sent between devices are 32-bit elements; how exact they have to be, the bound alone decides.
A program may use at most 64 MiB of HBM per device.

```python
import math
import jax
import jax.numpy as jnp
import numpy as np
from jax import lax

K = 128
DY = 2048
ROWS_DEV = 2048
FIRM_DEV = 128
PD_DEV = 16
CAP = 32
ROWS = 262144
N_ROWS = 128


def place_ends(values, own_key, smallest, top_value):
    longest = values.shape.index(max(values.shape))
    spots = []
    for shift in (0, 1):
        where = [jax.random.randint(jax.random.fold_in(own_key, axis), (), 0, length) for axis, length in enumerate(values.shape)]
        where[longest] = (where[longest] + shift) % values.shape[longest]
        spots.append(tuple(where))
    return values.at[spots[0]].set(smallest).at[spots[1]].set(top_value)


def strengthened(drawn, own_key, source, target, shards_of, factor):
    def block_of(axis_at):
        return (jnp.arange(drawn.shape[axis_at]) // (drawn.shape[axis_at] // shards_of)).reshape((-1,) + (1,) * (drawn.ndim - 1 - axis_at))

    near = jax.random.permutation(own_key, shards_of)[block_of(target)]
    other_side = (block_of(target) + shards_of // 2) % shards_of
    return jnp.where((block_of(source) == near) | (block_of(source) == other_side), factor * drawn, drawn)


def levels(rng, shape, cuts, least, top_value):
    level = 1.0
    for dim, parts in cuts:
        heights = jax.random.uniform(jax.random.fold_in(jax.random.fold_in(rng, 6), dim), (parts,), jnp.float32, least / len(cuts), top_value / len(cuts))
        level = level * jnp.repeat(jnp.exp(heights), shape[dim] // parts).reshape((-1,) + (1,) * (len(shape) - 1 - dim))
    return level


def rank_table(count, slope):
    portions = [(1 << 20) // math.isqrt(rank ** slope) + 1 for rank in range(1, count + 1)]
    deviation = 1 + sum(portions) // (1 << 30)
    return np.cumsum(np.array([max(1, weight // deviation) for weight in portions]))


def ranked_ids(stream_key, shape, amount, lean):
    listing = rank_table(amount, lean)
    lot = jax.random.randint(jax.random.fold_in(stream_key, 1), shape, 0, int(listing[amount - 1]))
    standing = jnp.searchsorted(jnp.asarray(listing, jnp.int32), lot, side="right")
    return jax.random.permutation(jax.random.fold_in(stream_key, 2), amount)[standing].astype(jnp.int32)


def assign_block(rng, own, number, rows, number_of, top, most, slope):
    order = jax.random.permutation(rng, number_of)
    heavy_load, common = portions_of(number_of, rows * top, most, slope, True), portions_of(number_of, rows * top, most, slope, False)
    places = jnp.arange(number_of)

    def named(sizes, turn):
        used = int((sizes > 0).sum())
        fixed = max(1, used // 4)
        shifted = fixed + (places - fixed + turn * (used - fixed)) % max(1, number_of - fixed)
        return jnp.zeros((number_of,), jnp.int32).at[order[jnp.where(places < fixed, places, shifted)]].set(jnp.asarray(sizes, jnp.int32))

    sizes = jnp.where(number % 4 == 0, named(heavy_load, number // 4), named(common, number - number // 4 - 1))
    mixed = jax.random.permutation(jax.random.fold_in(own, 3), number_of)
    giver, sink = mixed[0:number_of // 2 * 2:2], mixed[1:number_of // 2 * 2:2]
    room = jnp.minimum(sizes[giver] - 1, most - sizes[sink]) // 2
    room = jnp.where((giver == order[0]) | (sink == order[0]) | (sizes[sink] == 0), 0, jnp.maximum(room, 0))
    shifted = jax.random.randint(jax.random.fold_in(own, 4), (number_of // 2,), 0, 1 << 20) % (room + 1)
    sizes = sizes.at[giver].add(-shifted).at[sink].add(shifted)
    items = jnp.searchsorted(jnp.cumsum(sizes), jnp.arange(rows * top), side="right").astype(jnp.int32)
    listing = items.reshape(top, rows).T
    listing = listing[jax.random.permutation(jax.random.fold_in(own, 1), rows)]
    turn = jax.random.randint(jax.random.fold_in(own, 2), (rows, 1), 0, top)
    return jnp.take_along_axis(listing, (jnp.arange(top)[None, :] + turn) % top, axis=1)


def portions_of(amount, total, bound, lean, full):
    weights = [(1 << 20) // math.isqrt(rank ** lean) + 1 for rank in range(1, amount + 1)]
    largest = bound if full else min(bound, max(-(-total // amount), total * weights[0] // sum(weights)))
    least = 1 if total - largest >= amount - 1 else 0
    given, rest = [largest] + [least] * (amount - 1), total - largest - least * (amount - 1)
    while rest > 0:
        candidates = [i for i in range(1, amount) if given[i] < largest] or [i for i in range(1, amount) if given[i] < bound]
        pool, left = sum([weights[i] for i in candidates]), rest
        for i in candidates:
            addition = min(bound - given[i], max(1, left * weights[i] // pool), rest)
            given[i] = given[i] + addition
            rest = rest - addition
    return np.array(given)


def heavy_noise(rng, shape, deviation, reach, pieces, heavy, held_as=jnp.bfloat16):
    result = deviation * jax.random.normal(rng, shape, jnp.float32)
    if pieces:
        result = result * levels(rng, shape, pieces, -0.22, 0.18)
    return jnp.clip(strengthened(result, jax.random.fold_in(rng, 3), *heavy), -reach, reach).astype(held_as)


def setup_inputs(seed: int = 0) -> dict:
    key_of = jax.random.split(jax.random.key(seed), 8)
    covariates = heavy_noise(key_of[0], (ROWS, K), 1.0, 24.0, ((0, 128),), (0, 1, 128, 5.5), jnp.float32)
    outcome = jnp.clip(3.0 * jax.random.uniform(key_of[1], (ROWS,), jnp.float32) ** levels(key_of[1], (ROWS,), ((0, 128),), -0.2, 0.2), 0.0, 3.0)
    predictor = jnp.clip(jax.random.uniform(key_of[2], (ROWS,), jnp.float32, -1.5, 1.5) * levels(key_of[2], (ROWS,), ((0, 128),), -0.4, 0.0), -1.5, 1.5)
    firm_id = place_ends(jax.random.randint(key_of[3], (ROWS,), 0, FIRM_DEV), jax.random.fold_in(key_of[3], 1), 0, FIRM_DEV - 1).astype(jnp.int32)
    dy_id = place_ends(ranked_ids(key_of[4], (ROWS,), DY, 1), jax.random.fold_in(key_of[4], 3), 0, DY - 1).astype(jnp.int32)
    pd_owner_keys = jax.random.split(jax.random.fold_in(key_of[5], 1), ROWS // ROWS_DEV)
    pd_owner_turns = jax.random.permutation(jax.random.fold_in(key_of[5], 3), ROWS // ROWS_DEV)
    pd_owner = jax.vmap(lambda own, number: assign_block(jax.random.fold_in(key_of[5], 2), own, number, ROWS_DEV, N_ROWS, 1, CAP, 2))(pd_owner_keys, pd_owner_turns).reshape((ROWS, 1))
    pd_local = place_ends(ranked_ids(key_of[6], (ROWS,), PD_DEV, 2), jax.random.fold_in(key_of[6], 3), 0, PD_DEV - 1).astype(jnp.int32)
    return dict(covariates=covariates, outcome=outcome, predictor=predictor, firm_id=firm_id, dy_id=dy_id, pd_owner=pd_owner, pd_local=pd_local)


def center(values, weight, groups, segments):
    sum_w = jax.ops.segment_sum(weight, groups, num_segments=segments)
    sum_v = jax.ops.segment_sum(weight[:, None] * values, groups, num_segments=segments)
    denominator = jnp.where(sum_w > 0.0, sum_w, jnp.float32(1.0))
    mean_v = sum_v / denominator[:, None]
    return values - mean_v[groups]


def reference(covariates, outcome, predictor, firm_id, dy_id, pd_owner, pd_local):
    weight = jnp.exp(predictor)
    working = predictor + outcome / weight - 1.0
    shard_of = (jnp.arange(ROWS, dtype=jnp.int32) // ROWS_DEV).astype(jnp.int32)
    firm = (shard_of * FIRM_DEV + firm_id).astype(jnp.int32)
    effect = (pd_owner[:, 0] * PD_DEV + pd_local).astype(jnp.int32)
    values = jnp.concatenate([covariates, working[:, None]], axis=1)
    values = center(values, weight, firm, N_ROWS * FIRM_DEV)
    values = center(values, weight, dy_id, DY)
    values = center(values, weight, effect, N_ROWS * PD_DEV)
    x_tilde = values[:, :K]
    z_tilde = values[:, K]
    scaled = weight[:, None] * x_tilde
    gram = jnp.dot(scaled.T, x_tilde, precision=lax.Precision.HIGHEST) / ROWS
    rhs = jnp.dot(scaled.T, z_tilde, precision=lax.Precision.HIGHEST) / ROWS
    return x_tilde, z_tilde, gram, rhs
```

```python
import functools

import jax
import jax.numpy as jnp
from jax import lax
from jax.experimental import pallas as pl
from jax.experimental.pallas import tpu as pltpu
from jax.sharding import PartitionSpec as P

MESH = pl.DeviceIdType.MESH
F32 = jnp.float32
BF16 = jnp.bfloat16
I32 = jnp.int32
R = 2048
K = 128
NT = (((1,), (1,)), ((), ()))


def iota(shape, dim):
    return lax.broadcasted_iota(I32, shape, dim)


def split2(v):
    hi = v.astype(BF16)
    return hi, (v - hi.astype(F32)).astype(BF16)


def split3(v):
    hi = v.astype(BF16)
    rest = v - hi.astype(F32)
    mid = rest.astype(BF16)
    return hi, mid, (rest - mid.astype(F32)).astype(BF16)


def dot(a, b):
    return jnp.dot(a, b, preferred_element_type=F32)


def dot_nt(a, b):
    return lax.dot_general(a, b, NT, preferred_element_type=F32)


def blk(i, n=128):
    return slice(i * n, (i + 1) * n)


def kernel(total_rows, x_ref, out_r, pred_r, firm_r, dy_r, po_r, pl_r, pred_s, firm_s, dy_s, po_s, pl_s,
           xt_ref, zt_ref, gram_ref, rhs_ref, s):
    me = lax.axis_index("rows")
    c = lax.rem(me, 2)
    y = lax.rem(lax.div(me, 2), 4)
    x = lax.rem(lax.div(me, 8), 4)
    z = lax.div(me, 32)
    p = x + c * (y - x)
    q = y + c * (x - y)
    axis_p = (p, 8 - 6 * c)
    axis_q = (q, 2 + 6 * c)
    axis_z = (z, 32)
    partner = me + 1 - 2 * c
    mine = 64 * c
    theirs = 64 - mine

    def around(axis, k):
        u, stride = axis
        j = lax.rem(u + k, 4)
        return me + (j - u) * stride, j

    counter = [0]
    sends = []

    def sem(n=1):
        first = counter[0]
        counter[0] += n
        return first

    def remote(src, dst, device, slot):
        return pltpu.make_async_remote_copy(
            src_ref=src, dst_ref=dst, send_sem=s["send"].at[slot], recv_sem=s["recv"].at[slot],
            device_id=(device,), device_id_type=MESH)

    def push(src, dst, device):
        copy = remote(src, dst, device, sem())
        copy.start()
        sends.append(copy)
        return copy

    barrier = pltpu.get_barrier_semaphore()
    pl.semaphore_signal(barrier, inc=1, device_id=(partner,), device_id_type=MESH)
    for axis in (axis_p, axis_q, axis_z):
        for k in (1, 2, 3):
            pl.semaphore_signal(barrier, inc=1, device_id=(around(axis, k)[0],), device_id_type=MESH)

    dyf = dy_s[...].astype(F32)
    pdf = (po_s[...] * 16 + pl_s[...]).astype(F32)
    cols = jnp.transpose(jnp.concatenate(
        [jnp.exp(pred_s[...]), firm_s[...].astype(F32), dyf, pdf, jnp.zeros((64, 128), F32)], axis=0))
    lane = iota((128, 128), 1).astype(F32)
    for i in range(16):
        s["wc"][blk(i), :] = jnp.broadcast_to(cols[:, i:i + 1], (128, 128))
        s["fc"][blk(i), :] = (cols[:, 16 + i:17 + i] == lane).astype(F32).astype(BF16)
        s["dyc"][blk(i), :] = jnp.broadcast_to(cols[:, 32 + i:33 + i], (128, 128))
        s["pdc"][blk(i), :] = jnp.broadcast_to(cols[:, 48 + i:49 + i], (128, 128))

    @pl.loop(0, 4)
    def _(g):
        rows = pl.ds(pl.multiple_of(g * 512, 512), 512)
        hi, lo = split2(x_ref[rows, :] * s["wc"][rows, :])
        s["wv"][rows, 0:128] = hi
        s["wv"][rows, 128:256] = lo

    w_row = jnp.exp(pred_r[...])
    z_row = pred_r[...] + out_r[...] / w_row - 1.0
    wz_row = w_row * z_row
    firm_row = firm_r[...]
    sub = iota((128, 128), 0)
    acc_w = jnp.zeros((128, 128), F32)
    acc_z = jnp.zeros((128, 128), F32)
    for i in range(16):
        mask = jnp.broadcast_to(firm_row[:, blk(i)], (128, 128)) == sub
        s["ft"][:, blk(i)] = mask.astype(F32).astype(BF16)
        acc_w += jnp.where(mask, w_row[:, blk(i)], 0.0)
        acc_z += jnp.where(mask, wz_row[:, blk(i)], 0.0)
    firm_w = jnp.sum(acc_w, axis=1, keepdims=True)
    firm_z = jnp.sum(acc_z, axis=1, keepdims=True)
    den = jnp.where(firm_w > 0.0, firm_w, 1.0)
    firm_z = firm_z / den
    sums = dot(s["ft"][...], s["wv"][...])
    hi, lo = split2((sums[:, 0:128] + sums[:, 128:256]) / den)
    s["fm"][:, 0:128] = hi
    s["fm"][:, 128:256] = lo
    picks = []
    for i in range(16):
        mask = jnp.broadcast_to(firm_row[:, blk(i)], (128, 128)) == sub
        picks.append(jnp.sum(jnp.where(mask, firm_z, 0.0), axis=0, keepdims=True))
    z_row = z_row - jnp.concatenate(picks, axis=1)
    s["z"][...] = z_row
    wz_row = w_row * z_row

    @pl.loop(0, 4)
    def _(g):
        rows = pl.ds(pl.multiple_of(g * 512, 512), 512)
        got = dot(s["fc"][rows, :], s["fm"][...])
        v = x_ref[rows, :] - (got[:, 0:128] + got[:, 128:256])
        s["v"][rows, :] = v
        hi, lo = split2(v * s["wc"][rows, :])
        s["wv"][rows, 0:128] = hi
        s["wv"][rows, 128:256] = lo

    sub16 = iota((16, R), 0)

    def effects(own_row, loc_row, name):
        s[name + "_own"][...] = jnp.broadcast_to(own_row.astype(F32), (16, R)).astype(BF16)
        s[name + "_loc"][...] = (loc_row == sub16).astype(F32).astype(BF16)
        for i in range(16):
            s[name + "_ob"][:, blk(i)] = (
                jnp.broadcast_to(own_row[:, blk(i)], (128, 128)) == sub).astype(F32).astype(BF16)

    def table(name, slot):
        t_ref, got = s[name + "_t"], s[name + "_cr"]

        @pl.loop(0, 4)
        def _(it):
            base = lax.rem(theirs + it * 32, 128)
            for j in range(32):
                own = jnp.full((16, 128), 1.0, F32) * (base + j).astype(F32)
                own = jnp.concatenate([own.astype(BF16)] * 16, axis=1)
                s["lh"][blk(j, 16), :] = jnp.where(
                    s[name + "_own"][...] == own, s[name + "_loc"][...], jnp.zeros((16, R), BF16))
            sums = dot(s["lh"][...], s["wv"][...])
            t_ref[pl.ds(base, 32)] = (sums[:, 0:128] + sums[:, 128:256]).reshape(32, 16, 128)

            @pl.when(it < 2)
            def _():
                remote(t_ref.at[pl.ds(base, 32)], got.at[pl.ds(it * 32, 32)], partner, slot + it).start()

        for it in range(2):
            sends.append(remote(t_ref.at[pl.ds(theirs + it * 32, 32)], got.at[pl.ds(it * 32, 32)],
                                partner, slot + it))
        return sends[-2:]

    def scalar_sums(name, wz):
        hot = s[name + "_loc"][...].astype(F32)
        parts = []
        for row in (wz, w_row):
            for piece in split3(row):
                parts.append((hot * piece.astype(F32)).astype(BF16))
        e = dot_nt(jnp.concatenate(parts, axis=0), s[name + "_ob"][...])
        e = jnp.concatenate([e[0:16] + e[16:32] + e[32:48], e[48:64] + e[64:80] + e[80:96],
                             jnp.zeros((96, 128), F32)], axis=0)
        s[name + "_e"][...] = jnp.transpose(e).reshape(128, 1, 128)

    def rs_begin(name, axes):
        return {"n": name, "axes": axes, "live": None}

    def rs_send(job, stage):
        name, axis = job["n"], job["axes"][stage]
        part = (16, 4, 1)[stage]
        job["live"] = []
        for k in (1, 2, 3):
            device, j = around(axis, k)
            job["live"].append(push(s[f"{name}_a{stage}"].at[pl.ds(j * part, part)],
                                    s[f"{name}_r{stage}"].at[k - 1], device))

    def rs_wait(job, stage):
        name, (u, _) = job["n"], job["axes"][stage]
        part = (16, 4, 1)[stage]
        for copy in job["live"]:
            copy.wait_recv()
        got = s[f"{name}_r{stage}"]
        total = s[f"{name}_a{stage}"][pl.ds(u * part, part)] + got[0] + got[1] + got[2]
        if stage < 2:
            s[f"{name}_a{stage + 1}"][...] = total
        return total

    axes_dy = (axis_p, axis_q, axis_z)
    axes_pd = (axis_z, axis_p, axis_q)

    dy_row = dy_r[...]
    effects(lax.shift_right_logical(dy_row, 4), jnp.bitwise_and(dy_row, 15), "dy")
    pl.semaphore_wait(barrier, 10)
    dy_core = table("dy", sem(2))
    scalar_sums("dy", wz_row)
    dye_core = push(s["dy_e"].at[pl.ds(theirs, 64)], s["dy_ecr"], partner)
    for copy in dy_core:
        copy.wait_recv()
    s["dy_a0"][...] = s["dy_t"][pl.ds(mine, 64)] + s["dy_cr"][...]
    dy = rs_begin("dy", axes_dy)
    rs_send(dy, 0)
    dye_core.wait_recv()
    s["dye_a0"][...] = s["dy_e"][pl.ds(mine, 64)] + s["dy_ecr"][...]
    dye = rs_begin("dye", axes_dy)
    rs_send(dye, 0)

    po_row = po_r[...]
    pl_row = pl_r[...]
    effects(po_row, pl_row, "pd")
    upper = (iota((256, 256), 0) <= iota((256, 256), 1)).astype(F32).astype(BF16)
    carry = jnp.zeros((128, 1), F32)
    places = []
    for i in range(8):
        hot = s["pd_ob"][:, blk(i, 256)]
        run = dot(hot, upper) + carry
        carry = run[:, 255:256]
        places.append(jnp.sum(run * hot.astype(F32), axis=0, keepdims=True))
    place = jnp.concatenate(places, axis=1) - 1.0
    here = place == iota((32, R), 0).astype(F32)
    pieces = [lax.shift_right_logical(dy_row, 4).astype(F32), jnp.bitwise_and(dy_row, 15).astype(F32),
              pl_row.astype(F32)] + [v.astype(F32) for v in split3(w_row)]
    f = dot_nt(jnp.concatenate([jnp.where(here, v, 0.0).astype(BF16) for v in pieces], axis=0), s["pd_ob"][...])
    f = jnp.concatenate([f[0:32] * 16.0 + f[32:64], f[64:96], f[96:128] + f[128:160] + f[160:192],
                         jnp.zeros((32, 128), F32)], axis=0)
    s["f"][...] = jnp.transpose(f).reshape(128, 1, 128)
    f_live = [push(s["f"].at[pl.ds(theirs, 64)], s["f0"].at[1], partner)]
    s["f0"][0] = s["f"][pl.ds(mine, 64)]

    def f_send(stage):
        axis = axes_pd[stage]
        part = (16, 4, 1)[stage]
        src, dst = s[f"f{stage}"], s[f"f{stage + 1}"]
        pre = (slice(None),) * (stage + 1)
        f_live.clear()
        for k in (1, 2, 3):
            device, j = around(axis, k)
            f_live.append(push(src.at[pre + (pl.ds(j * part, part),)], dst.at[k], device))
        dst[0] = src[pre + (pl.ds(axis[0] * part, part),)]

    def f_wait():
        for copy in f_live:
            copy.wait_recv()

    pd_core = table("pd", sem(2))
    scalar_sums("pd", wz_row)
    pde_core = push(s["pd_e"].at[pl.ds(theirs, 64)], s["pd_ecr"], partner)

    rs_wait(dy, 0)
    rs_send(dy, 1)
    rs_wait(dye, 0)
    rs_send(dye, 1)
    for copy in pd_core:
        copy.wait_recv()
    s["pd_a0"][...] = s["pd_t"][pl.ds(mine, 64)] + s["pd_cr"][...]
    pd = rs_begin("pd", axes_pd)
    rs_send(pd, 0)
    pde_core.wait_recv()
    s["pde_a0"][...] = s["pd_e"][pl.ds(mine, 64)] + s["pd_ecr"][...]
    pde = rs_begin("pde", axes_pd)
    rs_send(pde, 0)
    f_wait()
    f_send(0)

    rs_wait(dy, 1)
    rs_send(dy, 2)
    rs_wait(dye, 1)
    rs_send(dye, 2)

    lane_id = iota((16, 128), 1)
    sub_id = iota((16, 128), 0)

    def column(e_row, first):
        spread = jnp.broadcast_to(e_row, (16, 128))
        return jnp.sum(jnp.where(lane_id == sub_id + first, spread, 0.0), axis=1, keepdims=True)

    def as_row(column16, first):
        spread = jnp.where(lane_id == sub_id + first, column16, 0.0)
        return jnp.sum(spread, axis=0, keepdims=True)

    def ag(name, block, row, order):
        full, fullz = s[name + "_m"], s[name + "_mz"]
        spots = {"p": p, "q": q, "z": z}
        own = [spots[a] for a in order]

        def view(fixed):
            index = [c] + [fixed[a] if a in fixed else slice(None) for a in order]
            return tuple(index)

        full[(c, *own)] = block
        fullz[(c, *own)] = row

        def stage(axis, fixed):
            out = []
            for k in (1, 2, 3):
                device, _ = around(axis, k)
                at = view(fixed)
                out.append((push(full.at[at], full.at[at], device), push(fullz.at[at], fullz.at[at], device)))
            return out

        def cross(fixed):
            at = view(fixed)
            return (push(full.at[at], full.at[at], partner), push(fullz.at[at], fullz.at[at], partner))

        def wait(copies):
            for pair in copies:
                for copy in pair:
                    copy.wait_recv()

        got = stage(axis_z, {"p": p, "q": q, "z": z})
        yield
        wait(got)
        got = stage(axis_q, {"p": p, "q": q})
        yield
        wait(got)
        got = stage(axis_p, {"p": p})
        last = [cross({"p": p})]
        yield
        for k in (1, 2, 3):
            wait([got[k - 1]])
            last.append(cross({"p": lax.rem(p + 4 - k, 4)}))
        yield
        wait(last)

    def onehot_cols(name):
        @pl.loop(0, 16)
        def _(i):
            rows = pl.ds(pl.multiple_of(i * 128, 128), 128)
            col = s[name + "c"][rows, :]
            for t in range(16):
                s[name + "_oh"][rows, blk(t)] = (col == lane + 128.0 * t).astype(F32).astype(BF16)

    onehot_cols("dy")

    block = rs_wait(dy, 2)[0]
    row = rs_wait(dye, 2)[0]
    w16 = column(row, 16)
    den = jnp.where(w16 > 0.0, w16, 1.0)
    lane_at = lax.rem(16 * c * 64 + 16 * (16 * p + 4 * q + z), 128)
    ag_dy = ag("dy", block / den, as_row(column(row, 0) / den, lane_at), ("p", "q", "z"))
    next(ag_dy)

    rs_wait(pd, 0)
    rs_send(pd, 1)
    rs_wait(pde, 0)
    rs_send(pde, 1)
    f_wait()
    f_send(1)
    next(ag_dy)
    onehot_cols("pd")
    next(ag_dy)
    rs_wait(pd, 1)
    rs_send(pd, 2)
    rs_wait(pde, 1)
    rs_send(pde, 2)
    f_wait()
    f_send(2)
    next(ag_dy)
    f_wait()

    rows_t = jnp.transpose(s["f3"][...].reshape(128, 128))
    dy_t = rows_t[0:32].astype(I32)
    high_t = lax.shift_right_logical(dy_t, 7) * 16 + rows_t[32:64].astype(I32)
    low_t = jnp.bitwise_and(dy_t, 127)
    w_hi, w_lo = split2(rows_t[64:96])
    w_hi, w_lo = w_hi.astype(F32), w_lo.astype(F32)
    sub256 = iota((256, 128), 0)
    pair = jnp.zeros((512, 128), F32)
    for g in range(4):
        for h in range(8):
            t = g * 8 + h
            there = jnp.broadcast_to(high_t[t:t + 1], (256, 128)) == sub256
            s["ml"][0:256, blk(h)] = jnp.where(there, w_hi[t:t + 1], 0.0).astype(BF16)
            s["ml"][256:512, blk(h)] = jnp.where(there, w_lo[t:t + 1], 0.0).astype(BF16)
            s["mr"][:, blk(h)] = (jnp.broadcast_to(low_t[t:t + 1], (128, 128)) == sub).astype(F32).astype(BF16)
        pair += dot_nt(s["ml"][...], s["mr"][...])
    pair = pair[0:256] + pair[256:512]
    p_hi, p_lo = split2(pair)
    m_lhs = jnp.concatenate(
        [jnp.concatenate([v[blk(a, 16)] for a in range(16)], axis=1) for v in (p_hi, p_lo)], axis=0)
    pd_block = rs_wait(pd, 2)[0]
    pd_row = rs_wait(pde, 2)[0]

    for _ in ag_dy:
        pass

    def halves(name):
        hi, lo = split2(s[name + "_m"][...].reshape(R, 128))
        s["mh"][:, 0:128] = hi
        s["mh"][:, 128:256] = lo
        return jnp.sum(s[name + "_mz"][...].reshape(16, 8, 128), axis=1)

    mz = halves("dy")
    mm = dot(m_lhs, s["mh"][...])
    mm = mm[0:16, 0:128] + mm[0:16, 128:256] + mm[16:32, 0:128]
    mmz = jnp.zeros((16, 128), F32)
    for a in range(16):
        mmz += pair[blk(a, 16)] * mz[a:a + 1]
    mmz = jnp.sum(mmz, axis=1, keepdims=True)
    w16 = column(pd_row, 16)
    den = jnp.where(w16 > 0.0, w16, 1.0)
    qx = (pd_block - mm) / den
    qz = (column(pd_row, 0) - mmz) / den
    lane_at = lax.rem(16 * c * 64 + 16 * (16 * z + 4 * p + q), 128)
    ag_pd = ag("pd", qx, as_row(qz, lane_at), ("z", "p", "q"))
    next(ag_pd)

    def pick(name, sink):
        @pl.loop(0, 4)
        def _(g):
            rows = pl.ds(pl.multiple_of(g * 512, 512), 512)
            got = dot(s[name + "_oh"][rows, :], s["mh"][...])
            sink[rows, :] = s["v"][rows, :] - (got[:, 0:128] + got[:, 128:256])

    def pick_z(index_row, mz):
        high = lax.shift_right_logical(index_row, 7)
        low = jnp.bitwise_and(index_row, 127)
        parts = jnp.concatenate([v.astype(F32) for v in split3(mz)], axis=0).astype(BF16)
        out = []
        for i in range(16):
            hot = (jnp.broadcast_to(low[:, blk(i)], (128, 128)) == sub).astype(F32).astype(BF16)
            got = dot(parts, hot)
            got = got[0:16] + got[16:32] + got[32:48]
            out.append(jnp.sum(jnp.where(high[:, blk(i)] == sub_id, got, 0.0), axis=0, keepdims=True))
        return jnp.concatenate(out, axis=1)

    pick("dy", s["v"])
    z_row = s["z"][...] - pick_z(dy_row, mz)
    next(ag_pd)

    for i in range(16):
        v = s["v"][blk(i), :]
        hi, lo = split2(v)
        s["vs"][blk(i), 0:128] = hi
        s["vs"][blk(i), 128:256] = lo
        hi, lo = split2(jnp.transpose(v * s["wc"][blk(i), :]))
        s["lg"][0:128, blk(i)] = hi
        s["lg"][128:256, blk(i)] = lo
    hi, lo = split2(w_row * z_row)
    row_id = iota((16, R), 0)
    s["lg"][256:272, :] = jnp.where(
        row_id == 0, hi.astype(F32), jnp.where(row_id == 1, lo.astype(F32), 0.0)).astype(BF16)
    g = dot(s["lg"][...], s["vs"][...])
    rhs_row = jnp.sum(g[256:272, 0:128] + g[256:272, 128:256], axis=0, keepdims=True)
    g = g[0:128, 0:128] + g[0:128, 128:256] + g[128:256, 0:128] + g[128:256, 128:256]
    wq = qx * w16
    g = g - lax.dot_general(wq, qx, (((0,), (0,)), ((), ())), precision=lax.Precision.HIGHEST,
                            preferred_element_type=F32)
    rhs_row = rhs_row - jnp.sum(wq * qz, axis=0, keepdims=True)
    eye = iota((128, 128), 0) == iota((128, 128), 1)
    rhs_col = jnp.sum(jnp.where(eye, rhs_row, 0.0), axis=1, keepdims=True)
    g = jnp.concatenate([g, jnp.broadcast_to(rhs_col, (128, 128))], axis=1)
    o = iota((128, 128), 0)
    oc, op = lax.shift_right_logical(o, 6), jnp.bitwise_and(lax.shift_right_logical(o, 4), 3)
    oq, oz = jnp.bitwise_and(lax.shift_right_logical(o, 2), 3), jnp.bitwise_and(o, 3)
    ox, oy = op + oc * (oq - op), oq + oc * (op - oq)
    order = (iota((128, 128), 1) == oz * 32 + ox * 8 + oy * 2 + oc).astype(F32).astype(BF16)
    s["g"][...] = sum(dot(order, v) for v in split3(g)).reshape(128, 1, 256)
    g_core = push(s["g"].at[pl.ds(theirs, 64)], s["g_cr"], partner)
    next(ag_pd)
    g_core.wait_recv()
    s["g_a0"][...] = s["g"][pl.ds(mine, 64)] + s["g_cr"][...]
    gram = rs_begin("g", axes_dy)
    rs_send(gram, 0)
    next(ag_pd)
    rs_wait(gram, 0)
    rs_send(gram, 1)
    for _ in ag_pd:
        pass
    mz = halves("pd")
    rs_wait(gram, 1)
    rs_send(gram, 2)
    pick("pd", xt_ref)
    zt_ref[...] = z_row - pick_z(po_row * 16 + pl_row, mz)
    g_row = rs_wait(gram, 2)[0] / total_rows
    gram_ref[...] = g_row[:, 0:128]
    rhs_ref[...] = g_row[:, 128:129]
    for copy in sends:
        copy.wait_send()


def scratch():
    v = pltpu.VMEM
    shapes = {
        "wc": v((R, 128), F32), "dyc": v((R, 128), F32), "pdc": v((R, 128), F32), "fc": v((R, 128), BF16),
        "ft": v((128, R), BF16), "fm": v((128, 256), BF16), "wv": v((R, 256), BF16), "v": v((R, 128), F32),
        "z": v((1, R), F32), "lh": v((512, R), BF16), "mh": v((R, 256), BF16),
        "dy_oh": v((R, 2048), BF16), "pd_oh": v((R, 2048), BF16),
        "ml": v((512, 1024), BF16), "mr": v((128, 1024), BF16), "vs": v((R, 256), BF16), "lg": v((272, R), BF16),
        "f": v((128, 1, 128), F32), "f0": v((2, 64, 1, 128), F32), "f1": v((4, 2, 16, 1, 128), F32),
        "f2": v((4, 4, 2, 4, 1, 128), F32), "f3": v((4, 4, 4, 2, 1, 1, 128), F32),
        "g": v((128, 1, 256), F32), "g_cr": v((64, 1, 256), F32),
    }
    for name in ("dy", "pd"):
        shapes[name + "_own"] = v((16, R), BF16)
        shapes[name + "_loc"] = v((16, R), BF16)
        shapes[name + "_ob"] = v((128, R), BF16)
        shapes[name + "_t"] = v((128, 16, 128), F32)
        shapes[name + "_cr"] = v((64, 16, 128), F32)
        shapes[name + "_e"] = v((128, 1, 128), F32)
        shapes[name + "_ecr"] = v((64, 1, 128), F32)
        shapes[name + "_m"] = v((2, 4, 4, 4, 16, 128), F32)
        shapes[name + "_mz"] = v((2, 4, 4, 4, 1, 128), F32)
    for name, tail in (("dy", (16, 128)), ("pd", (16, 128)), ("dye", (1, 128)), ("pde", (1, 128)), ("g", (1, 256))):
        for stage, part in enumerate((64, 16, 4)):
            shapes[f"{name}_a{stage}"] = v((part, *tail), F32)
            shapes[f"{name}_r{stage}"] = v((3, part // 4, *tail), F32)
    shapes["send"] = pltpu.SemaphoreType.DMA((160,))
    shapes["recv"] = pltpu.SemaphoreType.DMA((160,))
    return shapes


def shards(total_rows, covariates, outcome, predictor, firm_id, dy_id, pd_owner, pd_local):
    owner = pd_owner.reshape(R)
    rows = [v.reshape(1, R) for v in (outcome, predictor, firm_id, dy_id, owner, pd_local)]
    squares = [v.reshape(16, 128) for v in (predictor, firm_id, dy_id, owner, pd_local)]
    vmem = pl.BlockSpec(memory_space=pltpu.VMEM)
    xt, zt, gram, rhs = pl.pallas_call(
        functools.partial(kernel, total_rows),
        out_shape=(jax.ShapeDtypeStruct((R, 128), F32), jax.ShapeDtypeStruct((1, R), F32),
                   jax.ShapeDtypeStruct((1, 128), F32), jax.ShapeDtypeStruct((1, 1), F32)),
        in_specs=[vmem] * 12,
        out_specs=(vmem,) * 4,
        scratch_shapes=[scratch()],
        compiler_params=pltpu.CompilerParams(
            collective_id=0, has_side_effects=True, vmem_limit_bytes=63 * 1024 * 1024),
        name="demean",
    )(covariates, *rows, *squares)
    return xt, zt.reshape(R), gram, rhs.reshape(1)


def solution(mesh):
    specs = (P("rows", None), P("rows"), P("rows"), P("rows"), P("rows"), P("rows", None), P("rows"))
    out_specs = (P("rows", None), P("rows"), P("rows", None), P("rows"))
    return jax.shard_map(functools.partial(shards, float(R * 128)), mesh=mesh, in_specs=specs,
                         out_specs=out_specs, check_vma=False)
```

```python
import functools

import jax
import jax.numpy as jnp
from jax import lax
from jax.experimental import pallas as pl
from jax.experimental.pallas import tpu as pltpu
from jax.sharding import PartitionSpec as P

MESH = pl.DeviceIdType.MESH
F32 = jnp.float32
BF16 = jnp.bfloat16
I32 = jnp.int32
R = 2048
K = 128
NT = (((1,), (1,)), ((), ()))


def iota(shape, dim):
    return lax.broadcasted_iota(I32, shape, dim)


def split2(v):
    hi = v.astype(BF16)
    return hi, (v - hi.astype(F32)).astype(BF16)


def split3(v):
    hi = v.astype(BF16)
    rest = v - hi.astype(F32)
    mid = rest.astype(BF16)
    return hi, mid, (rest - mid.astype(F32)).astype(BF16)


def dot(a, b):
    return jnp.dot(a, b, preferred_element_type=F32)


def dot_nt(a, b):
    return lax.dot_general(a, b, NT, preferred_element_type=F32)


def blk(i, n=128):
    return slice(i * n, (i + 1) * n)


def kernel(total_rows, x_ref, out_r, pred_r, firm_r, dy_r, po_r, pl_r, pred_s, firm_s, dy_s, po_s, pl_s,
           xt_ref, zt_ref, gram_ref, rhs_ref, s):
    me = lax.axis_index("rows")
    c = lax.rem(me, 2)
    chip = lax.div(me, 2)
    z, x, y = lax.div(chip, 16), lax.rem(lax.div(chip, 4), 4), lax.rem(chip, 4)
    partner = me + 1 - 2 * c
    mine = 64 * c
    theirs = 64 - mine

    def far(offset):
        return sum(min(v, 4 - v) for v in offset)

    offsets = sorted([(a, b, d) for a in range(4) for b in range(4) for d in range(4) if (a, b, d) != (0, 0, 0)],
                     key=lambda v: -far(v))
    chips = [(lax.rem(z + a, 4) * 16 + lax.rem(x + b, 4) * 4 + lax.rem(y + d, 4), a * 16 + b * 4 + d)
             for a, b, d in offsets]

    counter = [0]
    sends = []

    def sem(n=1):
        first = counter[0]
        counter[0] += n
        return first

    def remote(src, dst, device, send, recv):
        return pltpu.make_async_remote_copy(
            src_ref=src, dst_ref=dst, send_sem=s["send"].at[send], recv_sem=s["recv"].at[recv],
            device_id=(device,), device_id_type=MESH)

    def wait_bytes(ref, which, slot):
        pltpu.make_async_copy(ref, ref, s[which].at[slot]).wait()

    def cross(src, dst):
        slot = sem()
        copy = remote(src, dst, partner, slot, slot)
        copy.start()
        sends.append(lambda: wait_bytes(src, "send", slot))
        return lambda: wait_bytes(dst, "recv", slot)

    def scatter(src, got):
        slot = sem()
        for j, offset in chips:
            remote(src.at[j], got.at[offset], 2 * j + c, slot, slot).start()
        got[0] = src[chip]
        sends.append(lambda: wait_bytes(got.at[pl.ds(1, 63)], "send", slot))
        return lambda: wait_bytes(got.at[pl.ds(1, 63)], "recv", slot)

    def gather(full, block):
        full[c, chip] = block
        send, recv = sem(), sem(4)
        for j, offset in chips:
            remote(full.at[c, chip], full.at[c, chip], 2 * j + c, send, recv + offset // 16).start()
        sends.append(lambda: wait_bytes(full.at[0, pl.ds(0, 63)], "send", send))
        yield
        waits = []
        for step in (0, 1, 3, 2):
            wait_bytes(full.at[0, pl.ds(0, 16 if step else 15)], "recv", recv + step)
            plane = pl.ds(16 * lax.rem(z + 4 - step, 4), 16)
            waits.append(cross(full.at[c, plane], full.at[c, plane]))
        yield
        for wait in waits:
            wait()

    barrier = pltpu.get_barrier_semaphore()
    pl.semaphore_signal(barrier, inc=1, device_id=(partner,), device_id_type=MESH)
    for j, _ in chips:
        pl.semaphore_signal(barrier, inc=1, device_id=(2 * j + c,), device_id_type=MESH)

    dyf = dy_s[...].astype(F32)
    pdf = (po_s[...] * 16 + pl_s[...]).astype(F32)
    cols = jnp.transpose(jnp.concatenate(
        [jnp.exp(pred_s[...]), firm_s[...].astype(F32), dyf, pdf, jnp.zeros((64, 128), F32)], axis=0))
    lane = iota((128, 128), 1).astype(F32)
    for i in range(16):
        s["wc"][blk(i), :] = jnp.broadcast_to(cols[:, i:i + 1], (128, 128))
        s["fc"][blk(i), :] = (cols[:, 16 + i:17 + i] == lane).astype(F32).astype(BF16)
        s["dyc"][blk(i), :] = jnp.broadcast_to(cols[:, 32 + i:33 + i], (128, 128))
        s["pdc"][blk(i), :] = jnp.broadcast_to(cols[:, 48 + i:49 + i], (128, 128))

    @pl.loop(0, 4)
    def _(g):
        rows = pl.ds(pl.multiple_of(g * 512, 512), 512)
        hi, lo = split2(x_ref[rows, :] * s["wc"][rows, :])
        s["wv"][rows, 0:128] = hi
        s["wv"][rows, 128:256] = lo

    w_row = jnp.exp(pred_r[...])
    z_row = pred_r[...] + out_r[...] / w_row - 1.0
    wz_row = w_row * z_row
    firm_row = firm_r[...]
    sub = iota((128, 128), 0)
    acc_w = jnp.zeros((128, 128), F32)
    acc_z = jnp.zeros((128, 128), F32)
    for i in range(16):
        mask = jnp.broadcast_to(firm_row[:, blk(i)], (128, 128)) == sub
        s["ft"][:, blk(i)] = mask.astype(F32).astype(BF16)
        acc_w += jnp.where(mask, w_row[:, blk(i)], 0.0)
        acc_z += jnp.where(mask, wz_row[:, blk(i)], 0.0)
    firm_w = jnp.sum(acc_w, axis=1, keepdims=True)
    firm_z = jnp.sum(acc_z, axis=1, keepdims=True)
    den = jnp.where(firm_w > 0.0, firm_w, 1.0)
    firm_z = firm_z / den
    sums = dot(s["ft"][...], s["wv"][...])
    hi, lo = split2((sums[:, 0:128] + sums[:, 128:256]) / den)
    s["fm"][:, 0:128] = hi
    s["fm"][:, 128:256] = lo
    picks = []
    for i in range(16):
        mask = jnp.broadcast_to(firm_row[:, blk(i)], (128, 128)) == sub
        picks.append(jnp.sum(jnp.where(mask, firm_z, 0.0), axis=0, keepdims=True))
    z_row = z_row - jnp.concatenate(picks, axis=1)
    s["z"][...] = z_row
    wz_row = w_row * z_row

    @pl.loop(0, 4)
    def _(g):
        rows = pl.ds(pl.multiple_of(g * 512, 512), 512)
        got = dot(s["fc"][rows, :], s["fm"][...])
        v = x_ref[rows, :] - (got[:, 0:128] + got[:, 128:256])
        s["v"][rows, :] = v
        hi, lo = split2(v * s["wc"][rows, :])
        s["wv"][rows, 0:128] = hi
        s["wv"][rows, 128:256] = lo

    sub16 = iota((16, R), 0)

    def effects(own_row, loc_row, name):
        s[name + "_own"][...] = jnp.broadcast_to(own_row.astype(F32), (16, R)).astype(BF16)
        s[name + "_loc"][...] = (loc_row == sub16).astype(F32).astype(BF16)
        for i in range(16):
            s[name + "_ob"][:, blk(i)] = (
                jnp.broadcast_to(own_row[:, blk(i)], (128, 128)) == sub).astype(F32).astype(BF16)

    def table(name):
        t_ref, got = s[name + "_t"], s[name + "_cr"]
        slot = sem(2)

        @pl.loop(0, 4)
        def _(it):
            base = lax.rem(theirs + it * 32, 128)
            for j in range(32):
                own = jnp.full((16, 128), 1.0, F32) * (base + j).astype(F32)
                own = jnp.concatenate([own.astype(BF16)] * 16, axis=1)
                s["lh"][blk(j, 16), :] = jnp.where(
                    s[name + "_own"][...] == own, s[name + "_loc"][...], jnp.zeros((16, R), BF16))
            sums = dot(s["lh"][...], s["wv"][...])
            t_ref[pl.ds(base, 32), 0:16] = (sums[:, 0:128] + sums[:, 128:256]).reshape(32, 16, 128)

            @pl.when(it < 2)
            def _():
                remote(t_ref.at[pl.ds(base, 32)], got.at[pl.ds(it * 32, 32)], partner, slot + it, slot + it).start()

        for it in range(2):
            sends.append(lambda it=it: wait_bytes(got.at[pl.ds(it * 32, 32)], "send", slot + it))
        for it in range(2):
            wait_bytes(got.at[pl.ds(it * 32, 32)], "recv", slot + it)

    def scalar_sums(name, wz):
        hot = s[name + "_loc"][...].astype(F32)
        parts = []
        for row in (wz, w_row):
            for piece in split3(row):
                parts.append((hot * piece.astype(F32)).astype(BF16))
        e = dot_nt(jnp.concatenate(parts, axis=0), s[name + "_ob"][...])
        e = jnp.concatenate([e[0:16] + e[16:32] + e[32:48], e[48:64] + e[64:80] + e[80:96],
                             jnp.zeros((96, 128), F32)], axis=0)
        s[name + "_t"][:, 16:17] = jnp.transpose(e).reshape(128, 1, 128)

    dy_row = dy_r[...]
    effects(lax.shift_right_logical(dy_row, 4), jnp.bitwise_and(dy_row, 15), "dy")
    scalar_sums("dy", wz_row)
    pl.semaphore_wait(barrier, 64)
    table("dy")
    s["dy_a"][...] = s["dy_t"][pl.ds(mine, 64)] + s["dy_cr"][...]
    dy_wait = scatter(s["dy_a"], s["dy_got"])

    po_row = po_r[...]
    pl_row = pl_r[...]
    effects(po_row, pl_row, "pd")
    upper = (iota((256, 256), 0) <= iota((256, 256), 1)).astype(F32).astype(BF16)
    carry = jnp.zeros((128, 1), F32)
    places = []
    for i in range(8):
        hot = s["pd_ob"][:, blk(i, 256)]
        run = dot(hot, upper) + carry
        carry = run[:, 255:256]
        places.append(jnp.sum(run * hot.astype(F32), axis=0, keepdims=True))
    place = jnp.concatenate(places, axis=1) - 1.0
    here = place == iota((32, R), 0).astype(F32)
    pieces = [lax.shift_right_logical(dy_row, 4).astype(F32), jnp.bitwise_and(dy_row, 15).astype(F32),
              pl_row.astype(F32)] + [v.astype(F32) for v in split3(w_row)]
    f = dot_nt(jnp.concatenate([jnp.where(here, v, 0.0).astype(BF16) for v in pieces], axis=0), s["pd_ob"][...])
    f = jnp.concatenate([f[0:32] * 16.0 + f[32:64], f[64:96], f[96:128] + f[128:160] + f[160:192],
                         jnp.zeros((32, 128), F32)], axis=0)
    s["pd_t"][:, 17:18] = jnp.transpose(f).reshape(128, 1, 128)
    scalar_sums("pd", wz_row)
    table("pd")
    s["pd_a"][:, 0:17] = s["pd_t"][pl.ds(mine, 64), 0:17] + s["pd_cr"][:, 0:17]
    s["pd_a"][:, 17:18] = s["pd_t"][pl.ds(mine, 64), 17:18]
    s["pd_a"][:, 18:19] = s["pd_cr"][:, 17:18]
    pd_wait = scatter(s["pd_a"], s["pd_got"])

    lane_id = iota((16, 128), 1)
    sub_id = iota((16, 128), 0)

    def column(e_row, first):
        spread = jnp.broadcast_to(e_row, (16, 128))
        return jnp.sum(jnp.where(lane_id == sub_id + first, spread, 0.0), axis=1, keepdims=True)

    def as_row(column16, first):
        spread = jnp.where(lane_id == sub_id + first, column16, 0.0)
        return jnp.sum(spread, axis=0, keepdims=True)

    def onehot_cols(name):
        @pl.loop(0, 16)
        def _(i):
            rows = pl.ds(pl.multiple_of(i * 128, 128), 128)
            col = s[name + "c"][rows, :]
            for t in range(16):
                s[name + "_oh"][rows, blk(t)] = (col == lane + 128.0 * t).astype(F32).astype(BF16)

    onehot_cols("dy")
    dy_wait()
    total = jnp.sum(s["dy_got"][...], axis=0)
    row = total[16:17]
    w16 = column(row, 16)
    den = jnp.where(w16 > 0.0, w16, 1.0)
    lane_at = 16 * lax.rem(chip, 8)
    ag_dy = gather(s["dy_m"], jnp.concatenate([total[0:16] / den, as_row(column(row, 0) / den, lane_at)], axis=0))
    next(ag_dy)
    onehot_cols("pd")
    pd_wait()

    rows_t = jnp.transpose(s["pd_got"][:, 17:19].reshape(128, 128))
    dy_t = rows_t[0:32].astype(I32)
    high_t = lax.shift_right_logical(dy_t, 7) * 16 + rows_t[32:64].astype(I32)
    low_t = jnp.bitwise_and(dy_t, 127)
    w_hi, w_lo = split2(rows_t[64:96])
    w_hi, w_lo = w_hi.astype(F32), w_lo.astype(F32)
    sub256 = iota((256, 128), 0)
    pair = jnp.zeros((512, 128), F32)
    for g in range(4):
        for h in range(8):
            t = g * 8 + h
            there = jnp.broadcast_to(high_t[t:t + 1], (256, 128)) == sub256
            s["ml"][0:256, blk(h)] = jnp.where(there, w_hi[t:t + 1], 0.0).astype(BF16)
            s["ml"][256:512, blk(h)] = jnp.where(there, w_lo[t:t + 1], 0.0).astype(BF16)
            s["mr"][:, blk(h)] = (jnp.broadcast_to(low_t[t:t + 1], (128, 128)) == sub).astype(F32).astype(BF16)
        pair += dot_nt(s["ml"][...], s["mr"][...])
    pair = pair[0:256] + pair[256:512]
    p_hi, p_lo = split2(pair)
    m_lhs = jnp.concatenate(
        [jnp.concatenate([v[blk(a, 16)] for a in range(16)], axis=1) for v in (p_hi, p_lo)], axis=0)
    pd_total = jnp.sum(s["pd_got"][:, 0:17], axis=0)
    pd_block, pd_row = pd_total[0:16], pd_total[16:17]

    for _ in ag_dy:
        pass

    def halves(name):
        hi, lo = split2(s[name + "_m"][:, :, 0:16].reshape(R, 128))
        s["mh"][:, 0:128] = hi
        s["mh"][:, 128:256] = lo
        return jnp.sum(s[name + "_m"][:, :, 16:17].reshape(16, 8, 128), axis=1)

    mz = halves("dy")
    mm = dot(m_lhs, s["mh"][...])
    mm = mm[0:16, 0:128] + mm[0:16, 128:256] + mm[16:32, 0:128]
    mmz = jnp.zeros((16, 128), F32)
    for a in range(16):
        mmz += pair[blk(a, 16)] * mz[a:a + 1]
    mmz = jnp.sum(mmz, axis=1, keepdims=True)
    w16 = column(pd_row, 16)
    den = jnp.where(w16 > 0.0, w16, 1.0)
    qx = (pd_block - mm) / den
    qz = (column(pd_row, 0) - mmz) / den
    ag_pd = gather(s["pd_m"], jnp.concatenate([qx, as_row(qz, lane_at)], axis=0))
    next(ag_pd)

    def pick(name, sink):
        @pl.loop(0, 4)
        def _(g):
            rows = pl.ds(pl.multiple_of(g * 512, 512), 512)
            got = dot(s[name + "_oh"][rows, :], s["mh"][...])
            sink[rows, :] = s["v"][rows, :] - (got[:, 0:128] + got[:, 128:256])

    def pick_z(index_row, mz):
        high = lax.shift_right_logical(index_row, 7)
        low = jnp.bitwise_and(index_row, 127)
        parts = jnp.concatenate([v.astype(F32) for v in split3(mz)], axis=0).astype(BF16)
        out = []
        for i in range(16):
            hot = (jnp.broadcast_to(low[:, blk(i)], (128, 128)) == sub).astype(F32).astype(BF16)
            got = dot(parts, hot)
            got = got[0:16] + got[16:32] + got[32:48]
            out.append(jnp.sum(jnp.where(high[:, blk(i)] == sub_id, got, 0.0), axis=0, keepdims=True))
        return jnp.concatenate(out, axis=1)

    pick("dy", s["v"])
    z_row = s["z"][...] - pick_z(dy_row, mz)

    for i in range(16):
        v = s["v"][blk(i), :]
        hi, lo = split2(v)
        s["vs"][blk(i), 0:128] = hi
        s["vs"][blk(i), 128:256] = lo
        hi, lo = split2(jnp.transpose(v * s["wc"][blk(i), :]))
        s["lg"][0:128, blk(i)] = hi
        s["lg"][128:256, blk(i)] = lo
    hi, lo = split2(w_row * z_row)
    row_id = iota((16, R), 0)
    s["lg"][256:272, :] = jnp.where(
        row_id == 0, hi.astype(F32), jnp.where(row_id == 1, lo.astype(F32), 0.0)).astype(BF16)
    g = dot(s["lg"][...], s["vs"][...])
    rhs_row = jnp.sum(g[256:272, 0:128] + g[256:272, 128:256], axis=0, keepdims=True)
    g = g[0:128, 0:128] + g[0:128, 128:256] + g[128:256, 0:128] + g[128:256, 128:256]
    wq = qx * w16
    g = g - lax.dot_general(wq, qx, (((0,), (0,)), ((), ())), precision=lax.Precision.HIGHEST,
                            preferred_element_type=F32)
    rhs_row = rhs_row - jnp.sum(wq * qz, axis=0, keepdims=True)
    eye = iota((128, 128), 0) == iota((128, 128), 1)
    rhs_col = jnp.sum(jnp.where(eye, rhs_row, 0.0), axis=1, keepdims=True)
    g = jnp.concatenate([g, jnp.broadcast_to(rhs_col, (128, 128))], axis=1)
    o = iota((128, 128), 0)
    device = 2 * jnp.bitwise_and(o, 63) + lax.shift_right_logical(o, 6)
    order = (iota((128, 128), 1) == device).astype(F32).astype(BF16)
    s["g"][...] = sum(dot(order, v) for v in split3(g)).reshape(128, 1, 256)
    g_wait = cross(s["g"].at[pl.ds(theirs, 64)], s["g_cr"])
    g_wait()
    s["g_a"][...] = s["g"][pl.ds(mine, 64)] + s["g_cr"][...]
    g_wait = scatter(s["g_a"], s["g_got"])
    for _ in ag_pd:
        pass
    mz = halves("pd")
    pick("pd", xt_ref)
    zt_ref[...] = z_row - pick_z(po_row * 16 + pl_row, mz)
    g_wait()
    g_row = jnp.sum(s["g_got"][...], axis=0) / total_rows
    gram_ref[...] = g_row[:, 0:128]
    rhs_ref[...] = g_row[:, 128:129]
    for wait in sends:
        wait()


def scratch():
    v = pltpu.VMEM
    shapes = {
        "wc": v((R, 128), F32), "dyc": v((R, 128), F32), "pdc": v((R, 128), F32), "fc": v((R, 128), BF16),
        "ft": v((128, R), BF16), "fm": v((128, 256), BF16), "wv": v((R, 256), BF16), "v": v((R, 128), F32),
        "z": v((1, R), F32), "lh": v((512, R), BF16), "mh": v((R, 256), BF16),
        "dy_oh": v((R, 2048), BF16), "pd_oh": v((R, 2048), BF16),
        "ml": v((512, 1024), BF16), "mr": v((128, 1024), BF16), "vs": v((R, 256), BF16), "lg": v((272, R), BF16),
        "g": v((128, 1, 256), F32), "g_cr": v((64, 1, 256), F32), "g_a": v((64, 1, 256), F32),
        "g_got": v((64, 1, 256), F32),
    }
    for name, extra in (("dy", 1), ("pd", 3)):
        sent = 16 + min(extra, 2)
        shapes[name + "_own"] = v((16, R), BF16)
        shapes[name + "_loc"] = v((16, R), BF16)
        shapes[name + "_ob"] = v((128, R), BF16)
        shapes[name + "_t"] = v((128, sent, 128), F32)
        shapes[name + "_cr"] = v((64, sent, 128), F32)
        shapes[name + "_a"] = v((64, 16 + extra, 128), F32)
        shapes[name + "_got"] = v((64, 16 + extra, 128), F32)
        shapes[name + "_m"] = v((2, 64, 17, 128), F32)
    shapes["send"] = pltpu.SemaphoreType.DMA((32,))
    shapes["recv"] = pltpu.SemaphoreType.DMA((32,))
    return shapes


def shards(total_rows, covariates, outcome, predictor, firm_id, dy_id, pd_owner, pd_local):
    owner = pd_owner.reshape(R)
    rows = [v.reshape(1, R) for v in (outcome, predictor, firm_id, dy_id, owner, pd_local)]
    squares = [v.reshape(16, 128) for v in (predictor, firm_id, dy_id, owner, pd_local)]
    vmem = pl.BlockSpec(memory_space=pltpu.VMEM)
    xt, zt, gram, rhs = pl.pallas_call(
        functools.partial(kernel, total_rows),
        out_shape=(jax.ShapeDtypeStruct((R, 128), F32), jax.ShapeDtypeStruct((1, R), F32),
                   jax.ShapeDtypeStruct((1, 128), F32), jax.ShapeDtypeStruct((1, 1), F32)),
        in_specs=[vmem] * 12,
        out_specs=(vmem,) * 4,
        scratch_shapes=[scratch()],
        compiler_params=pltpu.CompilerParams(
            collective_id=0, has_side_effects=True, vmem_limit_bytes=63 * 1024 * 1024),
        name="demean",
    )(covariates, *rows, *squares)
    return xt, zt.reshape(R), gram, rhs.reshape(1)


def solution(mesh):
    specs = (P("rows", None), P("rows"), P("rows"), P("rows"), P("rows"), P("rows", None), P("rows"))
    out_specs = (P("rows", None), P("rows"), P("rows", None), P("rows"))
    return jax.shard_map(functools.partial(shards, float(R * 128)), mesh=mesh, in_specs=specs,
                         out_specs=out_specs, check_vma=False)
```

```python
import functools

import jax
import jax.numpy as jnp
from jax import lax
from jax.experimental import pallas as pl
from jax.experimental.pallas import tpu as pltpu
from jax.sharding import PartitionSpec as P

MESH = pl.DeviceIdType.MESH
F32 = jnp.float32
BF16 = jnp.bfloat16
I32 = jnp.int32
R = 2048
K = 128
NT = (((1,), (1,)), ((), ()))


def iota(shape, dim):
    return lax.broadcasted_iota(I32, shape, dim)


def split2(v):
    hi = v.astype(BF16)
    return hi, (v - hi.astype(F32)).astype(BF16)


def split3(v):
    hi = v.astype(BF16)
    rest = v - hi.astype(F32)
    mid = rest.astype(BF16)
    return hi, mid, (rest - mid.astype(F32)).astype(BF16)


def dot(a, b):
    return jnp.dot(a, b, preferred_element_type=F32)


def dot_nt(a, b):
    return lax.dot_general(a, b, NT, preferred_element_type=F32)


def blk(i, n=128):
    return slice(i * n, (i + 1) * n)


def kernel(total_rows, x_ref, out_r, pred_r, firm_r, dy_r, po_r, pl_r, pred_s, firm_s, dy_s, po_s, pl_s,
           xt_ref, zt_ref, gram_ref, rhs_ref, s):
    me = lax.axis_index("rows")
    c = lax.rem(me, 2)
    y, x, z = lax.rem(lax.div(me, 2), 4), lax.rem(lax.div(me, 8), 4), lax.div(me, 32)
    p = x + c * (y - x)
    q = y + c * (x - y)
    place = p * 16 + q * 4 + z
    partner = me + 1 - 2 * c
    mine = 64 * c
    theirs = 64 - mine

    def far(offset):
        return sum(min(v, 4 - v) for v in offset)

    def at(a, b, d):
        pp, qq, zz = lax.rem(p + a, 4), lax.rem(q + b, 4), lax.rem(z + d, 4)
        return pp * 16 + qq * 4 + zz, c + pp * (8 - 6 * c) + qq * (2 + 6 * c) + zz * 32

    offsets = sorted([(a, b, d) for a in range(4) for b in range(4) for d in range(4) if (a, b, d) != (0, 0, 0)],
                     key=lambda v: -far(v))
    chips = [(*at(*v), v[0] * 16 + v[1] * 4 + v[2]) for v in offsets]

    counter = [0]
    sends = []

    def sem(n=1):
        first = counter[0]
        counter[0] += n
        return first

    def remote(src, dst, device, send, recv):
        return pltpu.make_async_remote_copy(
            src_ref=src, dst_ref=dst, send_sem=s["send"].at[send], recv_sem=s["recv"].at[recv],
            device_id=(device,), device_id_type=MESH)

    def wait_bytes(ref, which, slot):
        pltpu.make_async_copy(ref, ref, s[which].at[slot]).wait()

    def cross(src, dst):
        slot = sem()
        copy = remote(src, dst, partner, slot, slot)
        copy.start()
        sends.append(lambda: wait_bytes(src, "send", slot))
        return lambda: wait_bytes(dst, "recv", slot)

    def scatter(src, got):
        slot = sem()
        for j, device, offset in chips:
            remote(src.at[j], got.at[offset], device, slot, slot).start()
        got[0] = src[place]
        sends.append(lambda: wait_bytes(got.at[pl.ds(1, 63)], "send", slot))
        return lambda: wait_bytes(got.at[pl.ds(1, 63)], "recv", slot)

    def scatter_first(src, got):
        slot = sem()
        for k in (2, 1, 3):
            _, device = at(k, 0, 0)
            remote(src.at[pl.ds(16 * lax.rem(p + k, 4), 16)], got.at[k - 1], device, slot, slot).start()
        sends.append(lambda: wait_bytes(got, "send", slot))
        return lambda: wait_bytes(got, "recv", slot)

    def scatter_rest(src, got):
        slot = sem()
        plane = [v for v in offsets if v[0] == 0]
        for v in plane:
            j, device = at(*v)
            remote(src.at[lax.rem(j, 16)], got.at[v[1] * 4 + v[2]], device, slot, slot).start()
        got[0] = src[lax.rem(place, 16)]
        sends.append(lambda: wait_bytes(got.at[pl.ds(1, 15)], "send", slot))
        return lambda: wait_bytes(got.at[pl.ds(1, 15)], "recv", slot)

    def gather(full, block):
        full[c, place] = block
        send, recv = sem(), sem(4)
        for _, device, offset in chips:
            remote(full.at[c, place], full.at[c, place], device, send, recv + offset // 16).start()
        sends.append(lambda: wait_bytes(full.at[0, pl.ds(0, 63)], "send", send))
        yield None
        waits = []
        for step in (0, 1, 3, 2):
            wait_bytes(full.at[0, pl.ds(0, 16 if step else 15)], "recv", recv + step)
            first = lax.rem(p + 4 - step, 4)
            plane = pl.ds(16 * first, 16)
            waits.append(cross(full.at[c, plane], full.at[c, plane]))
            yield c, first
        for step, wait in zip((0, 1, 3, 2), waits):
            wait()
            yield 1 - c, lax.rem(q + 4 - step, 4)

    barrier = pltpu.get_barrier_semaphore()
    pl.semaphore_signal(barrier, inc=1, device_id=(partner,), device_id_type=MESH)
    for _, device, _ in chips:
        pl.semaphore_signal(barrier, inc=1, device_id=(device,), device_id_type=MESH)

    dyf = dy_s[...].astype(F32)
    pdf = (po_s[...] * 16 + pl_s[...]).astype(F32)
    cols = jnp.transpose(jnp.concatenate(
        [jnp.exp(pred_s[...]), firm_s[...].astype(F32), dyf, pdf, jnp.zeros((64, 128), F32)], axis=0))
    lane = iota((128, 128), 1).astype(F32)
    for i in range(16):
        s["wc"][blk(i), :] = jnp.broadcast_to(cols[:, i:i + 1], (128, 128))
        s["fc"][blk(i), :] = (cols[:, 16 + i:17 + i] == lane).astype(F32).astype(BF16)
        s["dyc"][blk(i), :] = jnp.broadcast_to(cols[:, 32 + i:33 + i], (128, 128))
        s["pdc"][blk(i), :] = jnp.broadcast_to(cols[:, 48 + i:49 + i], (128, 128))

    @pl.loop(0, 4)
    def _(g):
        rows = pl.ds(pl.multiple_of(g * 512, 512), 512)
        hi, lo = split2(x_ref[rows, :] * s["wc"][rows, :])
        s["wv"][rows, 0:128] = hi
        s["wv"][rows, 128:256] = lo

    w_row = jnp.exp(pred_r[...])
    z_row = pred_r[...] + out_r[...] / w_row - 1.0
    wz_row = w_row * z_row
    firm_row = firm_r[...]
    sub = iota((128, 128), 0)
    acc_w = jnp.zeros((128, 128), F32)
    acc_z = jnp.zeros((128, 128), F32)
    for i in range(16):
        mask = jnp.broadcast_to(firm_row[:, blk(i)], (128, 128)) == sub
        s["ft"][:, blk(i)] = mask.astype(F32).astype(BF16)
        acc_w += jnp.where(mask, w_row[:, blk(i)], 0.0)
        acc_z += jnp.where(mask, wz_row[:, blk(i)], 0.0)
    firm_w = jnp.sum(acc_w, axis=1, keepdims=True)
    firm_z = jnp.sum(acc_z, axis=1, keepdims=True)
    den = jnp.where(firm_w > 0.0, firm_w, 1.0)
    firm_z = firm_z / den
    sums = dot(s["ft"][...], s["wv"][...])
    hi, lo = split2((sums[:, 0:128] + sums[:, 128:256]) / den)
    s["fm"][:, 0:128] = hi
    s["fm"][:, 128:256] = lo
    picks = []
    for i in range(16):
        mask = jnp.broadcast_to(firm_row[:, blk(i)], (128, 128)) == sub
        picks.append(jnp.sum(jnp.where(mask, firm_z, 0.0), axis=0, keepdims=True))
    z_row = z_row - jnp.concatenate(picks, axis=1)
    s["z"][...] = z_row
    wz_row = w_row * z_row

    @pl.loop(0, 4)
    def _(g):
        rows = pl.ds(pl.multiple_of(g * 512, 512), 512)
        got = dot(s["fc"][rows, :], s["fm"][...])
        v = x_ref[rows, :] - (got[:, 0:128] + got[:, 128:256])
        s["v"][rows, :] = v
        hi, lo = split2(v * s["wc"][rows, :])
        s["wv"][rows, 0:128] = hi
        s["wv"][rows, 128:256] = lo

    sub16 = iota((16, R), 0)

    def effects(own_row, loc_row, name):
        s[name + "_own"][...] = jnp.broadcast_to(own_row.astype(F32), (16, R)).astype(BF16)
        s[name + "_loc"][...] = (loc_row == sub16).astype(F32).astype(BF16)
        for i in range(16):
            s[name + "_ob"][:, blk(i)] = (
                jnp.broadcast_to(own_row[:, blk(i)], (128, 128)) == sub).astype(F32).astype(BF16)

    def table(name):
        t_ref, got = s[name + "_t"], s[name + "_cr"]
        slot = sem(2)

        @pl.loop(0, 4)
        def _(it):
            base = lax.rem(theirs + it * 32, 128)
            for j in range(32):
                own = jnp.full((16, 128), 1.0, F32) * (base + j).astype(F32)
                own = jnp.concatenate([own.astype(BF16)] * 16, axis=1)
                s["lh"][blk(j, 16), :] = jnp.where(
                    s[name + "_own"][...] == own, s[name + "_loc"][...], jnp.zeros((16, R), BF16))
            sums = dot(s["lh"][...], s["wv"][...])
            t_ref[pl.ds(base, 32), 0:16] = (sums[:, 0:128] + sums[:, 128:256]).reshape(32, 16, 128)

            @pl.when(it < 2)
            def _():
                remote(t_ref.at[pl.ds(base, 32)], got.at[pl.ds(it * 32, 32)], partner, slot + it, slot + it).start()

        for it in range(2):
            sends.append(lambda it=it: wait_bytes(got.at[pl.ds(it * 32, 32)], "send", slot + it))
        for it in range(2):
            wait_bytes(got.at[pl.ds(it * 32, 32)], "recv", slot + it)

    def scalar_sums(name, wz):
        hot = s[name + "_loc"][...].astype(F32)
        parts = []
        for row in (wz, w_row):
            for piece in split3(row):
                parts.append((hot * piece.astype(F32)).astype(BF16))
        e = dot_nt(jnp.concatenate(parts, axis=0), s[name + "_ob"][...])
        e = jnp.concatenate([e[0:16] + e[16:32] + e[32:48], e[48:64] + e[64:80] + e[80:96],
                             jnp.zeros((96, 128), F32)], axis=0)
        s[name + "_t"][:, 16:17] = jnp.transpose(e).reshape(128, 1, 128)

    dy_row = dy_r[...]
    effects(lax.shift_right_logical(dy_row, 4), jnp.bitwise_and(dy_row, 15), "dy")
    scalar_sums("dy", wz_row)
    pl.semaphore_wait(barrier, 64)
    table("dy")
    s["dy_a"][...] = s["dy_t"][pl.ds(mine, 64)] + s["dy_cr"][...]
    dy_wait = scatter(s["dy_a"], s["dy_got"])

    po_row = po_r[...]
    pl_row = pl_r[...]
    effects(po_row, pl_row, "pd")
    upper = (iota((256, 256), 0) <= iota((256, 256), 1)).astype(F32).astype(BF16)
    carry = jnp.zeros((128, 1), F32)
    places = []
    for i in range(8):
        hot = s["pd_ob"][:, blk(i, 256)]
        run = dot(hot, upper) + carry
        carry = run[:, 255:256]
        places.append(jnp.sum(run * hot.astype(F32), axis=0, keepdims=True))
    here = jnp.concatenate(places, axis=1) - 1.0 == iota((32, R), 0).astype(F32)
    pieces = [lax.shift_right_logical(dy_row, 4).astype(F32), jnp.bitwise_and(dy_row, 15).astype(F32),
              pl_row.astype(F32)] + [v.astype(F32) for v in split3(w_row)]
    f = dot_nt(jnp.concatenate([jnp.where(here, v, 0.0).astype(BF16) for v in pieces], axis=0), s["pd_ob"][...])
    f = jnp.concatenate([f[0:32] * 16.0 + f[32:64], f[64:96], f[96:128] + f[128:160] + f[160:192],
                         jnp.zeros((32, 128), F32)], axis=0)
    s["f"][...] = jnp.transpose(f).reshape(128, 1, 128)
    f_wait = cross(s["f"].at[pl.ds(theirs, 64)], s["f_cr"])
    scalar_sums("pd", wz_row)
    table("pd")
    f_wait()
    s["f_a"][:, 0:1] = s["f"][pl.ds(mine, 64)]
    s["f_a"][:, 1:2] = s["f_cr"][...]
    f_wait = scatter(s["f_a"], s["f_got"])
    s["pd_a"][...] = s["pd_t"][pl.ds(mine, 64)] + s["pd_cr"][...]
    pd_wait = scatter_first(s["pd_a"], s["pd_first"])

    lane_id = iota((16, 128), 1)
    sub_id = iota((16, 128), 0)

    def column(e_row, first):
        spread = jnp.broadcast_to(e_row, (16, 128))
        return jnp.sum(jnp.where(lane_id == sub_id + first, spread, 0.0), axis=1, keepdims=True)

    def as_row(column16, first):
        spread = jnp.where(lane_id == sub_id + first, column16, 0.0)
        return jnp.sum(spread, axis=0, keepdims=True)

    def onehot_cols(name):
        @pl.loop(0, 16)
        def _(i):
            rows = pl.ds(pl.multiple_of(i * 128, 128), 128)
            col = s[name + "c"][rows, :]
            for t in range(16):
                s[name + "_oh"][t // 2, rows, blk(t % 2)] = (col == lane + 128.0 * t).astype(F32).astype(BF16)

    onehot_cols("dy")
    dy_wait()
    total = jnp.sum(s["dy_got"][...], axis=0)
    row = total[16:17]
    w16 = column(row, 16)
    den = jnp.where(w16 > 0.0, w16, 1.0)
    lane_at = 16 * lax.rem(place, 8)
    ag_dy = gather(s["dy_m"], jnp.concatenate([total[0:16] / den, as_row(column(row, 0) / den, lane_at)], axis=0))
    next(ag_dy)
    onehot_cols("pd")
    f_wait()

    rows_t = jnp.transpose(s["f_got"][...].reshape(128, 128))
    dy_t = rows_t[0:32].astype(I32)
    high_t = lax.shift_right_logical(dy_t, 7) * 16 + rows_t[32:64].astype(I32)
    low_t = jnp.bitwise_and(dy_t, 127)
    w_hi, w_lo = split2(rows_t[64:96])
    w_hi, w_lo = w_hi.astype(F32), w_lo.astype(F32)
    sub256 = iota((256, 128), 0)
    pair = jnp.zeros((512, 128), F32)
    for g in range(4):
        for h in range(8):
            t = g * 8 + h
            there = jnp.broadcast_to(high_t[t:t + 1], (256, 128)) == sub256
            s["ml"][0:256, blk(h)] = jnp.where(there, w_hi[t:t + 1], 0.0).astype(BF16)
            s["ml"][256:512, blk(h)] = jnp.where(there, w_lo[t:t + 1], 0.0).astype(BF16)
            s["mr"][:, blk(h)] = (jnp.broadcast_to(low_t[t:t + 1], (128, 128)) == sub).astype(F32).astype(BF16)
        pair += dot_nt(s["ml"][...], s["mr"][...])
    pair = pair[0:256] + pair[256:512]
    p_hi, p_lo = split2(pair)
    for k in range(8):
        s["mm"][k] = jnp.concatenate([jnp.concatenate([v[blk(2 * k, 16)], v[blk(2 * k + 1, 16)]], axis=1)
                                      for v in (p_hi, p_lo)], axis=0)
    pd_wait()
    part = pl.ds(16 * p, 16)
    s["pd_b"][...] = s["pd_a"][part] + s["pd_first"][0] + s["pd_first"][1] + s["pd_first"][2]
    pd_wait = scatter_rest(s["pd_b"], s["pd_got"])

    def plane_halves(name, half, first):
        k = 4 * half + first
        rows = pl.ds(pl.multiple_of(256 * k, 256), 256)
        owners = pl.ds(16 * first, 16)
        hi, lo = split2(s[name + "_m"][half, owners, 0:16].reshape(256, 128))
        s["mh"][rows, 0:128] = hi
        s["mh"][rows, 128:256] = lo
        s[name + "_mz"][k] = jnp.sum(s[name + "_m"][half, owners, 16:17].reshape(2, 8, 128), axis=1)
        return k, rows

    acc = jnp.zeros((32, 256), F32)
    for half, first in ag_dy:
        k, rows = plane_halves("dy", half, first)
        acc += dot(s["mm"][k], s["mh"][rows, :])
    mm = acc[0:16, 0:128] + acc[0:16, 128:256] + acc[16:32, 0:128]
    mz = s["dy_mz"][...].reshape(16, 128)
    mmz = jnp.zeros((16, 128), F32)
    for a in range(16):
        mmz += pair[blk(a, 16)] * mz[a:a + 1]
    mmz = jnp.sum(mmz, axis=1, keepdims=True)
    pd_wait()
    pd_total = jnp.sum(s["pd_got"][...], axis=0)
    pd_row = pd_total[16:17]
    w16 = column(pd_row, 16)
    den = jnp.where(w16 > 0.0, w16, 1.0)
    qx = (pd_total[0:16] - mm) / den
    qz = (column(pd_row, 0) - mmz) / den
    ag_pd = gather(s["pd_m"], jnp.concatenate([qx, as_row(qz, lane_at)], axis=0))
    next(ag_pd)

    @pl.loop(0, 4)
    def _(g):
        rows = pl.ds(pl.multiple_of(g * 512, 512), 512)
        got = jnp.zeros((512, 256), F32)
        for k in range(8):
            got += dot(s["dy_oh"][k, rows, :], s["mh"][blk(k, 256), :])
        v = s["v"][rows, :] - (got[:, 0:128] + got[:, 128:256])
        s["v"][rows, :] = v
        xt_ref[rows, :] = v

    def pick_z(index_row, mz):
        high = lax.shift_right_logical(index_row, 7)
        low = jnp.bitwise_and(index_row, 127)
        parts = jnp.concatenate([v.astype(F32) for v in split3(mz)], axis=0).astype(BF16)
        out = []
        for i in range(16):
            hot = (jnp.broadcast_to(low[:, blk(i)], (128, 128)) == sub).astype(F32).astype(BF16)
            got = dot(parts, hot)
            got = got[0:16] + got[16:32] + got[32:48]
            out.append(jnp.sum(jnp.where(high[:, blk(i)] == sub_id, got, 0.0), axis=0, keepdims=True))
        return jnp.concatenate(out, axis=1)

    z_row = s["z"][...] - pick_z(dy_row, mz)

    for i in range(16):
        v = s["v"][blk(i), :]
        hi, lo = split2(v)
        s["vs"][blk(i), 0:128] = hi
        s["vs"][blk(i), 128:256] = lo
        hi, lo = split2(jnp.transpose(v * s["wc"][blk(i), :]))
        s["lg"][0:128, blk(i)] = hi
        s["lg"][128:256, blk(i)] = lo
    hi, lo = split2(w_row * z_row)
    row_id = iota((16, R), 0)
    s["lg"][256:272, :] = jnp.where(
        row_id == 0, hi.astype(F32), jnp.where(row_id == 1, lo.astype(F32), 0.0)).astype(BF16)
    g = dot(s["lg"][...], s["vs"][...])
    rhs_row = jnp.sum(g[256:272, 0:128] + g[256:272, 128:256], axis=0, keepdims=True)
    g = g[0:128, 0:128] + g[0:128, 128:256] + g[128:256, 0:128] + g[128:256, 128:256]
    wq = qx * w16
    g = g - lax.dot_general(wq, qx, (((0,), (0,)), ((), ())), precision=lax.Precision.HIGHEST,
                            preferred_element_type=F32)
    rhs_row = rhs_row - jnp.sum(wq * qz, axis=0, keepdims=True)
    eye = iota((128, 128), 0) == iota((128, 128), 1)
    rhs_col = jnp.sum(jnp.where(eye, rhs_row, 0.0), axis=1, keepdims=True)
    g = jnp.concatenate([g, jnp.broadcast_to(rhs_col, (128, 128))], axis=1)
    o = iota((128, 128), 0)
    oc, op = lax.shift_right_logical(o, 6), jnp.bitwise_and(lax.shift_right_logical(o, 4), 3)
    oq, oz = jnp.bitwise_and(lax.shift_right_logical(o, 2), 3), jnp.bitwise_and(o, 3)
    device = oc + op * (8 - 6 * oc) + oq * (2 + 6 * oc) + oz * 32
    order = (iota((128, 128), 1) == device).astype(F32).astype(BF16)
    s["g"][...] = sum(dot(order, v) for v in split3(g)).reshape(128, 1, 256)
    g_wait = cross(s["g"].at[pl.ds(theirs, 64)], s["g_cr"])
    g_wait()
    s["g_a"][...] = s["g"][pl.ds(mine, 64)] + s["g_cr"][...]
    g_wait = scatter(s["g_a"], s["g_got"])
    for half, first in ag_pd:
        k, part = plane_halves("pd", half, first)

        @pl.loop(0, 4)
        def _(g):
            rows = pl.ds(pl.multiple_of(g * 512, 512), 512)
            got = dot(s["pd_oh"][k, rows, :], s["mh"][part, :])
            xt_ref[rows, :] -= got[:, 0:128] + got[:, 128:256]

    zt_ref[...] = z_row - pick_z(po_row * 16 + pl_row, s["pd_mz"][...].reshape(16, 128))
    g_wait()
    g_row = jnp.sum(s["g_got"][...], axis=0) / total_rows
    gram_ref[...] = g_row[:, 0:128]
    rhs_ref[...] = g_row[:, 128:129]
    for wait in sends:
        wait()


def scratch():
    v = pltpu.VMEM
    shapes = {
        "wc": v((R, 128), F32), "dyc": v((R, 128), F32), "pdc": v((R, 128), F32), "fc": v((R, 128), BF16),
        "ft": v((128, R), BF16), "fm": v((128, 256), BF16), "wv": v((R, 256), BF16), "v": v((R, 128), F32),
        "z": v((1, R), F32), "lh": v((512, R), BF16), "mh": v((R, 256), BF16),
        "dy_oh": v((8, R, 256), BF16), "pd_oh": v((8, R, 256), BF16), "mm": v((8, 32, 256), BF16),
        "f": v((128, 1, 128), F32), "f_cr": v((64, 1, 128), F32), "f_a": v((64, 2, 128), F32),
        "f_got": v((64, 2, 128), F32), "pd_first": v((3, 16, 17, 128), F32), "pd_b": v((16, 17, 128), F32),
        "ml": v((512, 1024), BF16), "mr": v((128, 1024), BF16), "vs": v((R, 256), BF16), "lg": v((272, R), BF16),
        "g": v((128, 1, 256), F32), "g_cr": v((64, 1, 256), F32), "g_a": v((64, 1, 256), F32),
        "g_got": v((64, 1, 256), F32),
    }
    for name, slots in (("dy", 64), ("pd", 16)):
        shapes[name + "_own"] = v((16, R), BF16)
        shapes[name + "_loc"] = v((16, R), BF16)
        shapes[name + "_ob"] = v((128, R), BF16)
        shapes[name + "_t"] = v((128, 17, 128), F32)
        shapes[name + "_cr"] = v((64, 17, 128), F32)
        shapes[name + "_a"] = v((64, 17, 128), F32)
        shapes[name + "_got"] = v((slots, 17, 128), F32)
        shapes[name + "_m"] = v((2, 64, 17, 128), F32)
        shapes[name + "_mz"] = v((8, 2, 128), F32)
    shapes["send"] = pltpu.SemaphoreType.DMA((32,))
    shapes["recv"] = pltpu.SemaphoreType.DMA((32,))
    return shapes


def shards(total_rows, covariates, outcome, predictor, firm_id, dy_id, pd_owner, pd_local):
    owner = pd_owner.reshape(R)
    rows = [v.reshape(1, R) for v in (outcome, predictor, firm_id, dy_id, owner, pd_local)]
    squares = [v.reshape(16, 128) for v in (predictor, firm_id, dy_id, owner, pd_local)]
    vmem = pl.BlockSpec(memory_space=pltpu.VMEM)
    xt, zt, gram, rhs = pl.pallas_call(
        functools.partial(kernel, total_rows),
        out_shape=(jax.ShapeDtypeStruct((R, 128), F32), jax.ShapeDtypeStruct((1, R), F32),
                   jax.ShapeDtypeStruct((1, 128), F32), jax.ShapeDtypeStruct((1, 1), F32)),
        in_specs=[vmem] * 12,
        out_specs=(vmem,) * 4,
        scratch_shapes=[scratch()],
        compiler_params=pltpu.CompilerParams(
            collective_id=0, has_side_effects=True, vmem_limit_bytes=63 * 1024 * 1024),
        name="demean",
    )(covariates, *rows, *squares)
    return xt, zt.reshape(R), gram, rhs.reshape(1)


def solution(mesh):
    specs = (P("rows", None), P("rows"), P("rows"), P("rows"), P("rows"), P("rows", None), P("rows"))
    out_specs = (P("rows", None), P("rows"), P("rows", None), P("rows"))
    return jax.shard_map(functools.partial(shards, float(R * 128)), mesh=mesh, in_specs=specs,
                         out_specs=out_specs, check_vma=False)
```

```python
import functools

import jax
import jax.numpy as jnp
from jax import lax
from jax.experimental import pallas as pl
from jax.experimental.pallas import tpu as pltpu
from jax.sharding import PartitionSpec as P

MESH = pl.DeviceIdType.MESH
F32 = jnp.float32
BF16 = jnp.bfloat16
I32 = jnp.int32
R = 2048
K = 128
NT = (((1,), (1,)), ((), ()))


def iota(shape, dim):
    return lax.broadcasted_iota(I32, shape, dim)


def split2(v):
    hi = v.astype(BF16)
    return hi, (v - hi.astype(F32)).astype(BF16)


def split3(v):
    hi = v.astype(BF16)
    rest = v - hi.astype(F32)
    mid = rest.astype(BF16)
    return hi, mid, (rest - mid.astype(F32)).astype(BF16)


def dot(a, b):
    return jnp.dot(a, b, preferred_element_type=F32)


def dot_nt(a, b):
    return lax.dot_general(a, b, NT, preferred_element_type=F32)


def blk(i, n=128):
    return slice(i * n, (i + 1) * n)


def kernel(total_rows, x_ref, out_r, pred_r, firm_r, dy_r, po_r, pl_r, pred_s, firm_s, dy_s, po_s, pl_s,
           xt_ref, zt_ref, gram_ref, rhs_ref, s):
    me = lax.axis_index("rows")
    c = lax.rem(me, 2)
    y, x, z = lax.rem(lax.div(me, 2), 4), lax.rem(lax.div(me, 8), 4), lax.div(me, 32)
    p = x + c * (y - x)
    q = y + c * (x - y)
    place = p * 16 + q * 4 + z
    partner = me + 1 - 2 * c
    mine = 64 * c
    theirs = 64 - mine

    def far(offset):
        return sum(min(v, 4 - v) for v in offset)

    def at(a, b, d):
        pp, qq, zz = lax.rem(p + a, 4), lax.rem(q + b, 4), lax.rem(z + d, 4)
        return pp * 16 + qq * 4 + zz, c + pp * (8 - 6 * c) + qq * (2 + 6 * c) + zz * 32

    offsets = sorted([(a, b, d) for a in range(4) for b in range(4) for d in range(4) if (a, b, d) != (0, 0, 0)],
                     key=lambda v: -far(v))
    chips = [(*at(*v), v[0] * 16 + v[1] * 4 + v[2]) for v in offsets]

    counter = [0]
    sends = []

    def sem(n=1):
        first = counter[0]
        counter[0] += n
        return first

    def remote(src, dst, device, send, recv):
        return pltpu.make_async_remote_copy(
            src_ref=src, dst_ref=dst, send_sem=s["send"].at[send], recv_sem=s["recv"].at[recv],
            device_id=(device,), device_id_type=MESH)

    def wait_bytes(ref, which, slot):
        pltpu.make_async_copy(ref, ref, s[which].at[slot]).wait()

    def cross(src, dst):
        slot = sem()
        copy = remote(src, dst, partner, slot, slot)
        copy.start()
        sends.append(lambda: wait_bytes(src, "send", slot))
        return lambda: wait_bytes(dst, "recv", slot)

    def scatter(src, got):
        slot = sem()
        for j, device, offset in chips:
            remote(src.at[j], got.at[offset], device, slot, slot).start()
        got[0] = src[place]
        sends.append(lambda: wait_bytes(got.at[pl.ds(1, 63)], "send", slot))
        return lambda: wait_bytes(got.at[pl.ds(1, 63)], "recv", slot)

    def scatter_first(src, got):
        slot = sem()
        for k in (2, 1, 3):
            _, device = at(k, 0, 0)
            remote(src.at[pl.ds(16 * lax.rem(p + k, 4), 16)], got.at[k - 1], device, slot, slot).start()
        sends.append(lambda: wait_bytes(got, "send", slot))
        return lambda: wait_bytes(got, "recv", slot)

    def scatter_rest(src, got):
        slot = sem()
        plane = [v for v in offsets if v[0] == 0]
        for v in plane:
            j, device = at(*v)
            remote(src.at[lax.rem(j, 16)], got.at[v[1] * 4 + v[2]], device, slot, slot).start()
        got[0] = src[lax.rem(place, 16)]
        sends.append(lambda: wait_bytes(got.at[pl.ds(1, 15)], "send", slot))
        return lambda: wait_bytes(got.at[pl.ds(1, 15)], "recv", slot)

    def gather(full, block):
        full[c, place] = block
        send, recv = sem(), sem(4)
        for _, device, offset in chips:
            remote(full.at[c, place], full.at[c, place], device, send, recv + offset // 16).start()
        sends.append(lambda: wait_bytes(full.at[0, pl.ds(0, 63)], "send", send))
        yield None
        waits = []
        for step in (0, 1, 3, 2):
            wait_bytes(full.at[0, pl.ds(0, 16 if step else 15)], "recv", recv + step)
            first = lax.rem(p + 4 - step, 4)
            plane = pl.ds(16 * first, 16)
            waits.append(cross(full.at[c, plane], full.at[c, plane]))
            yield c, first
        for step, wait in zip((0, 1, 3, 2), waits):
            wait()
            yield 1 - c, lax.rem(q + 4 - step, 4)

    barrier = pltpu.get_barrier_semaphore()
    pl.semaphore_signal(barrier, inc=1, device_id=(partner,), device_id_type=MESH)
    for _, device, _ in chips:
        pl.semaphore_signal(barrier, inc=1, device_id=(device,), device_id_type=MESH)

    dyf = dy_s[...].astype(F32)
    pdf = (po_s[...] * 16 + pl_s[...]).astype(F32)
    cols = jnp.transpose(jnp.concatenate(
        [jnp.exp(pred_s[...]), firm_s[...].astype(F32), dyf, pdf, jnp.zeros((64, 128), F32)], axis=0))
    lane = iota((128, 128), 1).astype(F32)
    for i in range(16):
        s["wc"][blk(i), :] = jnp.broadcast_to(cols[:, i:i + 1], (128, 128))
        s["fc"][blk(i), :] = (cols[:, 16 + i:17 + i] == lane).astype(F32).astype(BF16)
        s["dyc"][blk(i), :] = jnp.broadcast_to(cols[:, 32 + i:33 + i], (128, 128))
        s["pdc"][blk(i), :] = jnp.broadcast_to(cols[:, 48 + i:49 + i], (128, 128))

    @pl.loop(0, 4)
    def _(g):
        rows = pl.ds(pl.multiple_of(g * 512, 512), 512)
        hi, lo = split2(x_ref[rows, :] * s["wc"][rows, :])
        s["wv"][rows, 0:128] = hi
        s["wv"][rows, 128:256] = lo

    w_row = jnp.exp(pred_r[...])
    z_row = pred_r[...] + out_r[...] / w_row - 1.0
    wz_row = w_row * z_row
    firm_row = firm_r[...]
    sub = iota((128, 128), 0)
    acc_w = jnp.zeros((128, 128), F32)
    acc_z = jnp.zeros((128, 128), F32)
    for i in range(16):
        mask = jnp.broadcast_to(firm_row[:, blk(i)], (128, 128)) == sub
        s["ft"][:, blk(i)] = mask.astype(F32).astype(BF16)
        acc_w += jnp.where(mask, w_row[:, blk(i)], 0.0)
        acc_z += jnp.where(mask, wz_row[:, blk(i)], 0.0)
    firm_w = jnp.sum(acc_w, axis=1, keepdims=True)
    firm_z = jnp.sum(acc_z, axis=1, keepdims=True)
    den = jnp.where(firm_w > 0.0, firm_w, 1.0)
    firm_z = firm_z / den
    sums = dot(s["ft"][...], s["wv"][...])
    hi, lo = split2((sums[:, 0:128] + sums[:, 128:256]) / den)
    s["fm"][:, 0:128] = hi
    s["fm"][:, 128:256] = lo
    picks = []
    for i in range(16):
        mask = jnp.broadcast_to(firm_row[:, blk(i)], (128, 128)) == sub
        picks.append(jnp.sum(jnp.where(mask, firm_z, 0.0), axis=0, keepdims=True))
    z_row = z_row - jnp.concatenate(picks, axis=1)
    s["z"][...] = z_row
    wz_row = w_row * z_row

    @pl.loop(0, 4)
    def _(g):
        rows = pl.ds(pl.multiple_of(g * 512, 512), 512)
        got = dot(s["fc"][rows, :], s["fm"][...])
        v = x_ref[rows, :] - (got[:, 0:128] + got[:, 128:256])
        s["v"][rows, :] = v
        hi, lo = split2(v * s["wc"][rows, :])
        s["wv"][rows, 0:128] = hi
        s["wv"][rows, 128:256] = lo

    sub16 = iota((16, R), 0)

    def effects(own_row, loc_row, name):
        s[name + "_own"][...] = jnp.broadcast_to(own_row.astype(F32), (16, R)).astype(BF16)
        s[name + "_loc"][...] = (loc_row == sub16).astype(F32).astype(BF16)
        for i in range(16):
            s[name + "_ob"][:, blk(i)] = (
                jnp.broadcast_to(own_row[:, blk(i)], (128, 128)) == sub).astype(F32).astype(BF16)

    def table(name):
        t_ref, got = s[name + "_t"], s[name + "_cr"]
        slot = sem(2)

        @pl.loop(0, 4)
        def _(it):
            base = lax.rem(theirs + it * 32, 128)
            for j in range(32):
                own = jnp.full((16, 128), 1.0, F32) * (base + j).astype(F32)
                own = jnp.concatenate([own.astype(BF16)] * 16, axis=1)
                s["lh"][blk(j, 16), :] = jnp.where(
                    s[name + "_own"][...] == own, s[name + "_loc"][...], jnp.zeros((16, R), BF16))
            sums = dot(s["lh"][...], s["wv"][...])
            t_ref[pl.ds(base, 32), 0:16] = (sums[:, 0:128] + sums[:, 128:256]).reshape(32, 16, 128)

            @pl.when(it < 2)
            def _():
                remote(t_ref.at[pl.ds(base, 32)], got.at[pl.ds(it * 32, 32)], partner, slot + it, slot + it).start()

        for it in range(2):
            sends.append(lambda it=it: wait_bytes(got.at[pl.ds(it * 32, 32)], "send", slot + it))
        for it in range(2):
            wait_bytes(got.at[pl.ds(it * 32, 32)], "recv", slot + it)

    def scalar_sums(name, wz):
        hot = s[name + "_loc"][...].astype(F32)
        parts = []
        for row in (wz, w_row):
            for piece in split3(row):
                parts.append((hot * piece.astype(F32)).astype(BF16))
        e = dot_nt(jnp.concatenate(parts, axis=0), s[name + "_ob"][...])
        e = jnp.concatenate([e[0:16] + e[16:32] + e[32:48], e[48:64] + e[64:80] + e[80:96],
                             jnp.zeros((96, 128), F32)], axis=0)
        s[name + "_t"][:, 16:17] = jnp.transpose(e).reshape(128, 1, 128)

    dy_row = dy_r[...]
    effects(lax.shift_right_logical(dy_row, 4), jnp.bitwise_and(dy_row, 15), "dy")
    scalar_sums("dy", wz_row)
    pl.semaphore_wait(barrier, 64)
    table("dy")
    s["dy_a"][...] = s["dy_t"][pl.ds(mine, 64)] + s["dy_cr"][...]
    dy_wait = scatter(s["dy_a"], s["dy_got"])

    po_row = po_r[...]
    pl_row = pl_r[...]
    effects(po_row, pl_row, "pd")
    upper = (iota((256, 256), 0) <= iota((256, 256), 1)).astype(F32).astype(BF16)
    carry = jnp.zeros((128, 1), F32)
    places = []
    for i in range(8):
        hot = s["pd_ob"][:, blk(i, 256)]
        run = dot(hot, upper) + carry
        carry = run[:, 255:256]
        places.append(jnp.sum(run * hot.astype(F32), axis=0, keepdims=True))
    here = jnp.concatenate(places, axis=1) - 1.0 == iota((32, R), 0).astype(F32)
    pieces = [lax.shift_right_logical(dy_row, 4).astype(F32), jnp.bitwise_and(dy_row, 15).astype(F32),
              pl_row.astype(F32)] + [v.astype(F32) for v in split3(w_row)]
    f = dot_nt(jnp.concatenate([jnp.where(here, v, 0.0).astype(BF16) for v in pieces], axis=0), s["pd_ob"][...])
    f = jnp.concatenate([f[0:32] * 16.0 + f[32:64], f[64:96], f[96:128] + f[128:160] + f[160:192],
                         jnp.zeros((32, 128), F32)], axis=0)
    s["f"][...] = jnp.transpose(f).reshape(128, 1, 128)
    f_wait = cross(s["f"].at[pl.ds(theirs, 64)], s["f_cr"])
    scalar_sums("pd", wz_row)
    table("pd")
    f_wait()
    s["f_a"][:, 0:1] = s["f"][pl.ds(mine, 64)]
    s["f_a"][:, 1:2] = s["f_cr"][...]
    f_wait = scatter(s["f_a"], s["f_got"])
    s["pd_a"][...] = s["pd_t"][pl.ds(mine, 64)] + s["pd_cr"][...]
    pd_wait = scatter_first(s["pd_a"], s["pd_first"])

    lane_id = iota((16, 128), 1)
    sub_id = iota((16, 128), 0)

    def column(e_row, first):
        spread = jnp.broadcast_to(e_row, (16, 128))
        return jnp.sum(jnp.where(lane_id == sub_id + first, spread, 0.0), axis=1, keepdims=True)

    def as_row(column16, first):
        spread = jnp.where(lane_id == sub_id + first, column16, 0.0)
        return jnp.sum(spread, axis=0, keepdims=True)

    def onehot_cols(name):
        @pl.loop(0, 16)
        def _(i):
            rows = pl.ds(pl.multiple_of(i * 128, 128), 128)
            col = s[name + "c"][rows, :]
            for t in range(16):
                s[name + "_oh"][t // 2, rows, blk(t % 2)] = (col == lane + 128.0 * t).astype(F32).astype(BF16)

    onehot_cols("dy")

    for i in range(16):
        v = s["v"][blk(i), :]
        hi, lo = split2(v)
        s["vs"][blk(i), 0:128] = hi
        s["vs"][blk(i), 128:256] = lo
        hi, lo = split2(jnp.transpose(v * s["wc"][blk(i), :]))
        s["lg"][0:128, blk(i)] = hi
        s["lg"][128:256, blk(i)] = lo
    hi, lo = split2(wz_row)
    row_id = iota((16, R), 0)
    s["lg"][256:272, :] = jnp.where(
        row_id == 0, hi.astype(F32), jnp.where(row_id == 1, lo.astype(F32), 0.0)).astype(BF16)
    g = dot(s["lg"][...], s["vs"][...])
    rhs_row = jnp.sum(g[256:272, 0:128] + g[256:272, 128:256], axis=0, keepdims=True)
    g = g[0:128, 0:128] + g[0:128, 128:256] + g[128:256, 0:128] + g[128:256, 128:256]

    def outer(a, b):
        return lax.dot_general(a, b, (((0,), (0,)), ((), ())), precision=lax.Precision.HIGHEST,
                               preferred_element_type=F32)

    dy_wait()
    total = jnp.sum(s["dy_got"][...], axis=0)
    row = total[16:17]
    w16 = column(row, 16)
    den = jnp.where(w16 > 0.0, w16, 1.0)
    lane_at = 16 * lax.rem(place, 8)
    mx = total[0:16] / den
    m_z = column(row, 0) / den
    ag_dy = gather(s["dy_m"], jnp.concatenate([mx, as_row(m_z, lane_at)], axis=0))
    next(ag_dy)
    g = g - outer(mx * w16, mx)
    rhs_row = rhs_row - jnp.sum(mx * w16 * m_z, axis=0, keepdims=True)
    onehot_cols("pd")
    f_wait()

    rows_t = jnp.transpose(s["f_got"][...].reshape(128, 128))
    dy_t = rows_t[0:32].astype(I32)
    high_t = lax.shift_right_logical(dy_t, 7) * 16 + rows_t[32:64].astype(I32)
    low_t = jnp.bitwise_and(dy_t, 127)
    w_hi, w_lo = split2(rows_t[64:96])
    w_hi, w_lo = w_hi.astype(F32), w_lo.astype(F32)
    sub256 = iota((256, 128), 0)
    pair = jnp.zeros((512, 128), F32)
    for step in range(4):
        for h in range(8):
            t = step * 8 + h
            there = jnp.broadcast_to(high_t[t:t + 1], (256, 128)) == sub256
            s["ml"][0:256, blk(h)] = jnp.where(there, w_hi[t:t + 1], 0.0).astype(BF16)
            s["ml"][256:512, blk(h)] = jnp.where(there, w_lo[t:t + 1], 0.0).astype(BF16)
            s["mr"][:, blk(h)] = (jnp.broadcast_to(low_t[t:t + 1], (128, 128)) == sub).astype(F32).astype(BF16)
        pair += dot_nt(s["ml"][...], s["mr"][...])
    pair = pair[0:256] + pair[256:512]
    p_hi, p_lo = split2(pair)
    for k in range(8):
        s["mm"][k] = jnp.concatenate([jnp.concatenate([v[blk(2 * k, 16)], v[blk(2 * k + 1, 16)]], axis=1)
                                      for v in (p_hi, p_lo)], axis=0)
    pd_wait()
    part = pl.ds(16 * p, 16)
    s["pd_b"][...] = s["pd_a"][part] + s["pd_first"][0] + s["pd_first"][1] + s["pd_first"][2]
    pd_wait = scatter_rest(s["pd_b"], s["pd_got"])

    def plane_halves(name, half, first):
        k = 4 * half + first
        rows = pl.ds(pl.multiple_of(256 * k, 256), 256)
        owners = pl.ds(16 * first, 16)
        hi, lo = split2(s[name + "_m"][half, owners, 0:16].reshape(256, 128))
        s["mh"][rows, 0:128] = hi
        s["mh"][rows, 128:256] = lo
        s[name + "_mz"][k] = jnp.sum(s[name + "_m"][half, owners, 16:17].reshape(2, 8, 128), axis=1)
        return k, rows

    acc = jnp.zeros((32, 256), F32)
    for half, first in ag_dy:
        k, rows = plane_halves("dy", half, first)
        acc += dot(s["mm"][k], s["mh"][rows, :])
    mm = acc[0:16, 0:128] + acc[0:16, 128:256] + acc[16:32, 0:128]
    mz = s["dy_mz"][...].reshape(16, 128)
    mmz = jnp.zeros((16, 128), F32)
    for a in range(16):
        mmz += pair[blk(a, 16)] * mz[a:a + 1]
    mmz = jnp.sum(mmz, axis=1, keepdims=True)
    pd_wait()
    pd_total = jnp.sum(s["pd_got"][...], axis=0)
    pd_row = pd_total[16:17]
    w16 = column(pd_row, 16)
    den = jnp.where(w16 > 0.0, w16, 1.0)
    qx = (pd_total[0:16] - mm) / den
    qz = (column(pd_row, 0) - mmz) / den
    ag_pd = gather(s["pd_m"], jnp.concatenate([qx, as_row(qz, lane_at)], axis=0))
    next(ag_pd)
    g = g - outer(qx * w16, qx)
    rhs_row = rhs_row - jnp.sum(qx * w16 * qz, axis=0, keepdims=True)
    eye = iota((128, 128), 0) == iota((128, 128), 1)
    rhs_col = jnp.sum(jnp.where(eye, rhs_row, 0.0), axis=1, keepdims=True)
    g = jnp.concatenate([g, jnp.broadcast_to(rhs_col, (128, 128))], axis=1)
    o = iota((128, 128), 0)
    oc, op = lax.shift_right_logical(o, 6), jnp.bitwise_and(lax.shift_right_logical(o, 4), 3)
    oq, oz = jnp.bitwise_and(lax.shift_right_logical(o, 2), 3), jnp.bitwise_and(o, 3)
    device = oc + op * (8 - 6 * oc) + oq * (2 + 6 * oc) + oz * 32
    order = (iota((128, 128), 1) == device).astype(F32).astype(BF16)
    s["g"][...] = sum(dot(order, v) for v in split3(g)).reshape(128, 1, 256)
    g_wait = cross(s["g"].at[pl.ds(theirs, 64)], s["g_cr"])
    g_wait()
    s["g_a"][...] = s["g"][pl.ds(mine, 64)] + s["g_cr"][...]
    g_wait = scatter(s["g_a"], s["g_got"])

    @pl.loop(0, 4)
    def _(g):
        rows = pl.ds(pl.multiple_of(g * 512, 512), 512)
        got = jnp.zeros((512, 256), F32)
        for k in range(8):
            got += dot(s["dy_oh"][k, rows, :], s["mh"][blk(k, 256), :])
        xt_ref[rows, :] = s["v"][rows, :] - (got[:, 0:128] + got[:, 128:256])

    def pick_z(index_row, mz):
        high = lax.shift_right_logical(index_row, 7)
        low = jnp.bitwise_and(index_row, 127)
        parts = jnp.concatenate([v.astype(F32) for v in split3(mz)], axis=0).astype(BF16)
        out = []
        for i in range(16):
            hot = (jnp.broadcast_to(low[:, blk(i)], (128, 128)) == sub).astype(F32).astype(BF16)
            got = dot(parts, hot)
            got = got[0:16] + got[16:32] + got[32:48]
            out.append(jnp.sum(jnp.where(high[:, blk(i)] == sub_id, got, 0.0), axis=0, keepdims=True))
        return jnp.concatenate(out, axis=1)

    z_row = s["z"][...] - pick_z(dy_row, mz)

    def pick_half(half):
        @pl.loop(0, 4)
        def _(g):
            rows = pl.ds(pl.multiple_of(g * 512, 512), 512)
            got = jnp.zeros((512, 256), F32)
            for j in range(4):
                part = pl.ds(pl.multiple_of(1024 * half + 256 * j, 256), 256)
                got += dot(s["pd_oh"][4 * half + j, rows, :], s["mh"][part, :])
            xt_ref[rows, :] -= got[:, 0:128] + got[:, 128:256]

    for i, (half, first) in enumerate(ag_pd):
        plane_halves("pd", half, first)
        if i in (3, 7):
            pick_half(half)

    zt_ref[...] = z_row - pick_z(po_row * 16 + pl_row, s["pd_mz"][...].reshape(16, 128))
    g_wait()
    g_row = jnp.sum(s["g_got"][...], axis=0) / total_rows
    gram_ref[...] = g_row[:, 0:128]
    rhs_ref[...] = g_row[:, 128:129]
    for wait in sends:
        wait()


def scratch():
    v = pltpu.VMEM
    shapes = {
        "wc": v((R, 128), F32), "dyc": v((R, 128), F32), "pdc": v((R, 128), F32), "fc": v((R, 128), BF16),
        "ft": v((128, R), BF16), "fm": v((128, 256), BF16), "wv": v((R, 256), BF16), "v": v((R, 128), F32),
        "z": v((1, R), F32), "lh": v((512, R), BF16), "mh": v((R, 256), BF16),
        "dy_oh": v((8, R, 256), BF16), "pd_oh": v((8, R, 256), BF16), "mm": v((8, 32, 256), BF16),
        "f": v((128, 1, 128), F32), "f_cr": v((64, 1, 128), F32), "f_a": v((64, 2, 128), F32),
        "f_got": v((64, 2, 128), F32), "pd_first": v((3, 16, 17, 128), F32), "pd_b": v((16, 17, 128), F32),
        "ml": v((512, 1024), BF16), "mr": v((128, 1024), BF16), "vs": v((R, 256), BF16), "lg": v((272, R), BF16),
        "g": v((128, 1, 256), F32), "g_cr": v((64, 1, 256), F32), "g_a": v((64, 1, 256), F32),
        "g_got": v((64, 1, 256), F32),
    }
    for name, slots in (("dy", 64), ("pd", 16)):
        shapes[name + "_own"] = v((16, R), BF16)
        shapes[name + "_loc"] = v((16, R), BF16)
        shapes[name + "_ob"] = v((128, R), BF16)
        shapes[name + "_t"] = v((128, 17, 128), F32)
        shapes[name + "_cr"] = v((64, 17, 128), F32)
        shapes[name + "_a"] = v((64, 17, 128), F32)
        shapes[name + "_got"] = v((slots, 17, 128), F32)
        shapes[name + "_m"] = v((2, 64, 17, 128), F32)
        shapes[name + "_mz"] = v((8, 2, 128), F32)
    shapes["send"] = pltpu.SemaphoreType.DMA((32,))
    shapes["recv"] = pltpu.SemaphoreType.DMA((32,))
    return shapes


def shards(total_rows, covariates, outcome, predictor, firm_id, dy_id, pd_owner, pd_local):
    owner = pd_owner.reshape(R)
    rows = [v.reshape(1, R) for v in (outcome, predictor, firm_id, dy_id, owner, pd_local)]
    squares = [v.reshape(16, 128) for v in (predictor, firm_id, dy_id, owner, pd_local)]
    vmem = pl.BlockSpec(memory_space=pltpu.VMEM)
    xt, zt, gram, rhs = pl.pallas_call(
        functools.partial(kernel, total_rows),
        out_shape=(jax.ShapeDtypeStruct((R, 128), F32), jax.ShapeDtypeStruct((1, R), F32),
                   jax.ShapeDtypeStruct((1, 128), F32), jax.ShapeDtypeStruct((1, 1), F32)),
        in_specs=[vmem] * 12,
        out_specs=(vmem,) * 4,
        scratch_shapes=[scratch()],
        compiler_params=pltpu.CompilerParams(
            collective_id=0, has_side_effects=True, vmem_limit_bytes=63 * 1024 * 1024),
        name="demean",
    )(covariates, *rows, *squares)
    return xt, zt.reshape(R), gram, rhs.reshape(1)


def solution(mesh):
    specs = (P("rows", None), P("rows"), P("rows"), P("rows"), P("rows"), P("rows", None), P("rows"))
    out_specs = (P("rows", None), P("rows"), P("rows", None), P("rows"))
    return jax.shard_map(functools.partial(shards, float(R * 128)), mesh=mesh, in_specs=specs,
                         out_specs=out_specs, check_vma=False)
```

```python
import functools

import jax
import jax.numpy as jnp
from jax import lax
from jax.experimental import pallas as pl
from jax.experimental.pallas import tpu as pltpu
from jax.sharding import PartitionSpec as P

MESH = pl.DeviceIdType.MESH
F32 = jnp.float32
BF16 = jnp.bfloat16
I32 = jnp.int32
R = 2048
K = 128
NT = (((1,), (1,)), ((), ()))


def iota(shape, dim):
    return lax.broadcasted_iota(I32, shape, dim)


def split2(v):
    hi = v.astype(BF16)
    return hi, (v - hi.astype(F32)).astype(BF16)


def split3(v):
    hi = v.astype(BF16)
    rest = v - hi.astype(F32)
    mid = rest.astype(BF16)
    return hi, mid, (rest - mid.astype(F32)).astype(BF16)


def dot(a, b):
    return jnp.dot(a, b, preferred_element_type=F32)


def dot_nt(a, b):
    return lax.dot_general(a, b, NT, preferred_element_type=F32)


def blk(i, n=128):
    return slice(i * n, (i + 1) * n)


def kernel(total_rows, x_ref, out_r, pred_r, firm_r, dy_r, po_r, pl_r, pred_s, firm_s, dy_s, po_s, pl_s,
           xt_ref, zt_ref, gram_ref, rhs_ref, s):
    me = lax.axis_index("rows")
    c = lax.rem(me, 2)
    y, x, z = lax.rem(lax.div(me, 2), 4), lax.rem(lax.div(me, 8), 4), lax.div(me, 32)
    p = x + c * (y - x)
    q = y + c * (x - y)
    place = p * 16 + q * 4 + z
    partner = me + 1 - 2 * c
    mine = 64 * c
    theirs = 64 - mine

    def far(offset):
        return sum(min(v, 4 - v) for v in offset)

    def at(a, b, d):
        pp, qq, zz = lax.rem(p + a, 4), lax.rem(q + b, 4), lax.rem(z + d, 4)
        return pp * 16 + qq * 4 + zz, c + pp * (8 - 6 * c) + qq * (2 + 6 * c) + zz * 32

    offsets = sorted([(a, b, d) for a in range(4) for b in range(4) for d in range(4) if (a, b, d) != (0, 0, 0)],
                     key=lambda v: -far(v))
    chips = [(*at(*v), v[0] * 16 + v[1] * 4 + v[2]) for v in offsets]

    counter = [0]
    sends = []

    def sem(n=1):
        first = counter[0]
        counter[0] += n
        return first

    def remote(src, dst, device, send, recv):
        return pltpu.make_async_remote_copy(
            src_ref=src, dst_ref=dst, send_sem=s["send"].at[send], recv_sem=s["recv"].at[recv],
            device_id=(device,), device_id_type=MESH)

    def wait_bytes(ref, which, slot):
        pltpu.make_async_copy(ref, ref, s[which].at[slot]).wait()

    def cross(src, dst):
        slot = sem()
        copy = remote(src, dst, partner, slot, slot)
        copy.start()
        sends.append(lambda: wait_bytes(src, "send", slot))
        return lambda: wait_bytes(dst, "recv", slot)

    def scatter(src, got):
        slot = sem()
        for j, device, offset in chips:
            remote(src.at[j], got.at[offset], device, slot, slot).start()
        got[0] = src[place]
        sends.append(lambda: wait_bytes(got.at[pl.ds(1, 63)], "send", slot))
        return lambda: wait_bytes(got.at[pl.ds(1, 63)], "recv", slot)

    def scatter_first(src, got):
        slot = sem()
        for k in (2, 1, 3):
            _, device = at(k, 0, 0)
            remote(src.at[pl.ds(16 * lax.rem(p + k, 4), 16)], got.at[k - 1], device, slot, slot).start()
        sends.append(lambda: wait_bytes(got, "send", slot))
        return lambda: wait_bytes(got, "recv", slot)

    def scatter_rest(src, got):
        slot = sem()
        plane = [v for v in offsets if v[0] == 0]
        for v in plane:
            j, device = at(*v)
            remote(src.at[lax.rem(j, 16)], got.at[v[1] * 4 + v[2]], device, slot, slot).start()
        got[0] = src[lax.rem(place, 16)]
        sends.append(lambda: wait_bytes(got.at[pl.ds(1, 15)], "send", slot))
        return lambda: wait_bytes(got.at[pl.ds(1, 15)], "recv", slot)

    def gather(full, block):
        full[c, place] = block
        send, recv = sem(), sem(4)
        for _, device, offset in chips:
            remote(full.at[c, place], full.at[c, place], device, send, recv + offset // 16).start()
        sends.append(lambda: wait_bytes(full.at[0, pl.ds(0, 63)], "send", send))
        yield None
        waits = []
        for step in (0, 1, 3, 2):
            wait_bytes(full.at[0, pl.ds(0, 16 if step else 15)], "recv", recv + step)
            first = lax.rem(p + 4 - step, 4)
            plane = pl.ds(16 * first, 16)
            waits.append(cross(full.at[c, plane], full.at[c, plane]))
            yield c, first
        for step, wait in zip((0, 1, 3, 2), waits):
            wait()
            yield 1 - c, lax.rem(q + 4 - step, 4)

    barrier = pltpu.get_barrier_semaphore()
    pl.semaphore_signal(barrier, inc=1, device_id=(partner,), device_id_type=MESH)
    for _, device, _ in chips:
        pl.semaphore_signal(barrier, inc=1, device_id=(device,), device_id_type=MESH)

    dyf = dy_s[...].astype(F32)
    pdf = (po_s[...] * 16 + pl_s[...]).astype(F32)
    cols = jnp.transpose(jnp.concatenate(
        [jnp.exp(pred_s[...]), firm_s[...].astype(F32), dyf, pdf, jnp.zeros((64, 128), F32)], axis=0))
    lane = iota((128, 128), 1).astype(F32)
    for i in range(16):
        s["wc"][blk(i), :] = jnp.broadcast_to(cols[:, i:i + 1], (128, 128))
        s["fc"][blk(i), :] = (cols[:, 16 + i:17 + i] == lane).astype(F32).astype(BF16)
        s["dyc"][blk(i), :] = jnp.broadcast_to(cols[:, 32 + i:33 + i], (128, 128))
        s["pdc"][blk(i), :] = jnp.broadcast_to(cols[:, 48 + i:49 + i], (128, 128))

    @pl.loop(0, 4)
    def _(g):
        rows = pl.ds(pl.multiple_of(g * 512, 512), 512)
        hi, lo = split2(x_ref[rows, :] * s["wc"][rows, :])
        s["wv"][rows, 0:128] = hi
        s["wv"][rows, 128:256] = lo

    w_row = jnp.exp(pred_r[...])
    z_row = pred_r[...] + out_r[...] / w_row - 1.0
    wz_row = w_row * z_row
    firm_row = firm_r[...]
    sub = iota((128, 128), 0)
    acc_w = jnp.zeros((128, 128), F32)
    acc_z = jnp.zeros((128, 128), F32)
    for i in range(16):
        mask = jnp.broadcast_to(firm_row[:, blk(i)], (128, 128)) == sub
        s["ft"][:, blk(i)] = mask.astype(F32).astype(BF16)
        acc_w += jnp.where(mask, w_row[:, blk(i)], 0.0)
        acc_z += jnp.where(mask, wz_row[:, blk(i)], 0.0)
    firm_w = jnp.sum(acc_w, axis=1, keepdims=True)
    firm_z = jnp.sum(acc_z, axis=1, keepdims=True)
    den = jnp.where(firm_w > 0.0, firm_w, 1.0)
    firm_z = firm_z / den
    sums = dot(s["ft"][...], s["wv"][...])
    hi, lo = split2((sums[:, 0:128] + sums[:, 128:256]) / den)
    s["fm"][:, 0:128] = hi
    s["fm"][:, 128:256] = lo
    picks = []
    for i in range(16):
        mask = jnp.broadcast_to(firm_row[:, blk(i)], (128, 128)) == sub
        picks.append(jnp.sum(jnp.where(mask, firm_z, 0.0), axis=0, keepdims=True))
    z_row = z_row - jnp.concatenate(picks, axis=1)
    s["z"][...] = z_row
    wz_row = w_row * z_row

    @pl.loop(0, 4)
    def _(g):
        rows = pl.ds(pl.multiple_of(g * 512, 512), 512)
        got = dot(s["fc"][rows, :], s["fm"][...])
        v = x_ref[rows, :] - (got[:, 0:128] + got[:, 128:256])
        s["v"][rows, :] = v
        hi, lo = split2(v * s["wc"][rows, :])
        s["wv"][rows, 0:128] = hi
        s["wv"][rows, 128:256] = lo

    sub16 = iota((16, R), 0)

    def effects(own_row, loc_row, name):
        s[name + "_own"][...] = jnp.broadcast_to(own_row.astype(F32), (16, R)).astype(BF16)
        s[name + "_loc"][...] = (loc_row == sub16).astype(F32).astype(BF16)
        for i in range(16):
            s[name + "_ob"][:, blk(i)] = (
                jnp.broadcast_to(own_row[:, blk(i)], (128, 128)) == sub).astype(F32).astype(BF16)

    def table(name):
        t_ref, got = s[name + "_t"], s[name + "_cr"]
        slot = sem(2)

        @pl.loop(0, 4)
        def _(it):
            base = lax.rem(theirs + it * 32, 128)
            for j in range(32):
                own = jnp.full((16, 128), 1.0, F32) * (base + j).astype(F32)
                own = jnp.concatenate([own.astype(BF16)] * 16, axis=1)
                s["lh"][blk(j, 16), :] = jnp.where(
                    s[name + "_own"][...] == own, s[name + "_loc"][...], jnp.zeros((16, R), BF16))
            sums = dot(s["lh"][...], s["wv"][...])
            t_ref[pl.ds(base, 32), 0:16] = (sums[:, 0:128] + sums[:, 128:256]).reshape(32, 16, 128)

            @pl.when(it < 2)
            def _():
                remote(t_ref.at[pl.ds(base, 32)], got.at[pl.ds(it * 32, 32)], partner, slot + it, slot + it).start()

        for it in range(2):
            sends.append(lambda it=it: wait_bytes(got.at[pl.ds(it * 32, 32)], "send", slot + it))
        for it in range(2):
            wait_bytes(got.at[pl.ds(it * 32, 32)], "recv", slot + it)

    def scalar_sums(name, wz):
        hot = s[name + "_loc"][...].astype(F32)
        parts = []
        for row in (wz, w_row):
            for piece in split3(row):
                parts.append((hot * piece.astype(F32)).astype(BF16))
        e = dot_nt(jnp.concatenate(parts, axis=0), s[name + "_ob"][...])
        e = jnp.concatenate([e[0:16] + e[16:32] + e[32:48], e[48:64] + e[64:80] + e[80:96],
                             jnp.zeros((96, 128), F32)], axis=0)
        s[name + "_t"][:, 16:17] = jnp.transpose(e).reshape(128, 1, 128)

    dy_row = dy_r[...]
    effects(lax.shift_right_logical(dy_row, 4), jnp.bitwise_and(dy_row, 15), "dy")
    scalar_sums("dy", wz_row)
    pl.semaphore_wait(barrier, 64)
    table("dy")
    s["dy_a"][...] = s["dy_t"][pl.ds(mine, 64)] + s["dy_cr"][...]
    dy_wait = scatter(s["dy_a"], s["dy_got"])

    po_row = po_r[...]
    pl_row = pl_r[...]
    effects(po_row, pl_row, "pd")
    upper = (iota((256, 256), 0) <= iota((256, 256), 1)).astype(F32).astype(BF16)
    carry = jnp.zeros((128, 1), F32)
    places = []
    for i in range(8):
        hot = s["pd_ob"][:, blk(i, 256)]
        run = dot(hot, upper) + carry
        carry = run[:, 255:256]
        places.append(jnp.sum(run * hot.astype(F32), axis=0, keepdims=True))
    here = jnp.concatenate(places, axis=1) - 1.0 == iota((32, R), 0).astype(F32)
    pieces = [lax.shift_right_logical(dy_row, 4).astype(F32), jnp.bitwise_and(dy_row, 15).astype(F32),
              pl_row.astype(F32)] + [v.astype(F32) for v in split3(w_row)]
    f = dot_nt(jnp.concatenate([jnp.where(here, v, 0.0).astype(BF16) for v in pieces], axis=0), s["pd_ob"][...])
    f = jnp.concatenate([f[0:32] * 16.0 + f[32:64], f[64:96], f[96:128] + f[128:160] + f[160:192],
                         jnp.zeros((32, 128), F32)], axis=0)
    s["f"][...] = jnp.transpose(f).reshape(128, 1, 128)
    f_wait = cross(s["f"].at[pl.ds(theirs, 64)], s["f_cr"])
    scalar_sums("pd", wz_row)
    table("pd")
    f_wait()
    s["f_a"][:, 0:1] = s["f"][pl.ds(mine, 64)]
    s["f_a"][:, 1:2] = s["f_cr"][...]
    f_wait = scatter(s["f_a"], s["f_got"])
    s["pd_a"][...] = s["pd_t"][pl.ds(mine, 64)] + s["pd_cr"][...]
    pd_wait = scatter_first(s["pd_a"], s["pd_first"])

    lane_id = iota((16, 128), 1)
    sub_id = iota((16, 128), 0)

    def column(e_row, first):
        spread = jnp.broadcast_to(e_row, (16, 128))
        return jnp.sum(jnp.where(lane_id == sub_id + first, spread, 0.0), axis=1, keepdims=True)

    def as_row(column16, first):
        spread = jnp.where(lane_id == sub_id + first, column16, 0.0)
        return jnp.sum(spread, axis=0, keepdims=True)

    def onehot_cols(name):
        @pl.loop(0, 16)
        def _(i):
            rows = pl.ds(pl.multiple_of(i * 128, 128), 128)
            col = s[name + "c"][rows, :]
            for t in range(16):
                s[name + "_oh"][t // 2, rows, blk(t % 2)] = (col == lane + 128.0 * t).astype(F32).astype(BF16)

    onehot_cols("dy")

    for i in range(16):
        v = s["v"][blk(i), :]
        hi, lo = split2(v)
        s["vs"][blk(i), 0:128] = hi
        s["vs"][blk(i), 128:256] = lo
        hi, lo = split2(jnp.transpose(v * s["wc"][blk(i), :]))
        s["lg"][0:128, blk(i)] = hi
        s["lg"][128:256, blk(i)] = lo
    hi, lo = split2(wz_row)
    row_id = iota((16, R), 0)
    s["lg"][256:272, :] = jnp.where(
        row_id == 0, hi.astype(F32), jnp.where(row_id == 1, lo.astype(F32), 0.0)).astype(BF16)
    g = dot(s["lg"][...], s["vs"][...])
    rhs_row = jnp.sum(g[256:272, 0:128] + g[256:272, 128:256], axis=0, keepdims=True)
    g = g[0:128, 0:128] + g[0:128, 128:256] + g[128:256, 0:128] + g[128:256, 128:256]

    def outer(a, b):
        return lax.dot_general(a, b, (((0,), (0,)), ((), ())), precision=lax.Precision.HIGHEST,
                               preferred_element_type=F32)

    dy_wait()
    total = jnp.sum(s["dy_got"][...], axis=0)
    row = total[16:17]
    w16 = column(row, 16)
    den = jnp.where(w16 > 0.0, w16, 1.0)
    lane_at = 16 * lax.rem(place, 8)
    mx = total[0:16] / den
    m_z = column(row, 0) / den
    ag_dy = gather(s["dy_m"], jnp.concatenate([mx, as_row(m_z, lane_at)], axis=0))
    next(ag_dy)
    g = g - outer(mx * w16, mx)
    rhs_row = rhs_row - jnp.sum(mx * w16 * m_z, axis=0, keepdims=True)
    onehot_cols("pd")
    f_wait()

    rows_t = jnp.transpose(s["f_got"][...].reshape(128, 128))
    dy_t = rows_t[0:32].astype(I32)
    high_t = lax.shift_right_logical(dy_t, 7) * 16 + rows_t[32:64].astype(I32)
    low_t = jnp.bitwise_and(dy_t, 127)
    w_hi, w_lo = split2(rows_t[64:96])
    w_hi, w_lo = w_hi.astype(F32), w_lo.astype(F32)
    sub256 = iota((256, 128), 0)
    pair = jnp.zeros((512, 128), F32)
    for step in range(4):
        for h in range(8):
            t = step * 8 + h
            there = jnp.broadcast_to(high_t[t:t + 1], (256, 128)) == sub256
            s["ml"][0:256, blk(h)] = jnp.where(there, w_hi[t:t + 1], 0.0).astype(BF16)
            s["ml"][256:512, blk(h)] = jnp.where(there, w_lo[t:t + 1], 0.0).astype(BF16)
            s["mr"][:, blk(h)] = (jnp.broadcast_to(low_t[t:t + 1], (128, 128)) == sub).astype(F32).astype(BF16)
        pair += dot_nt(s["ml"][...], s["mr"][...])
    pair = pair[0:256] + pair[256:512]
    p_hi, p_lo = split2(pair)
    for k in range(8):
        s["mm"][k] = jnp.concatenate([jnp.concatenate([v[blk(2 * k, 16)], v[blk(2 * k + 1, 16)]], axis=1)
                                      for v in (p_hi, p_lo)], axis=0)
    pd_wait()
    part = pl.ds(16 * p, 16)
    s["pd_b"][...] = s["pd_a"][part] + s["pd_first"][0] + s["pd_first"][1] + s["pd_first"][2]
    pd_wait = scatter_rest(s["pd_b"], s["pd_got"])

    def plane_halves(name, half, first):
        k = 4 * half + first
        rows = pl.ds(pl.multiple_of(256 * k, 256), 256)
        owners = pl.ds(16 * first, 16)
        hi, lo = split2(s[name + "_m"][half, owners, 0:16].reshape(256, 128))
        s["mh"][rows, 0:128] = hi
        s["mh"][rows, 128:256] = lo
        s[name + "_mz"][k] = jnp.sum(s[name + "_m"][half, owners, 16:17].reshape(2, 8, 128), axis=1)
        return k, rows

    acc = jnp.zeros((32, 256), F32)
    for half, first in ag_dy:
        k, rows = plane_halves("dy", half, first)
        acc += dot(s["mm"][k], s["mh"][rows, :])
    mm = acc[0:16, 0:128] + acc[0:16, 128:256] + acc[16:32, 0:128]
    mz = s["dy_mz"][...].reshape(16, 128)
    mmz = jnp.zeros((16, 128), F32)
    for a in range(16):
        mmz += pair[blk(a, 16)] * mz[a:a + 1]
    mmz = jnp.sum(mmz, axis=1, keepdims=True)
    pd_wait()
    pd_total = jnp.sum(s["pd_got"][...], axis=0)
    pd_row = pd_total[16:17]
    w16 = column(pd_row, 16)
    den = jnp.where(w16 > 0.0, w16, 1.0)
    qx = (pd_total[0:16] - mm) / den
    qz = (column(pd_row, 0) - mmz) / den
    ag_pd = gather(s["pd_m"], jnp.concatenate([qx, as_row(qz, lane_at)], axis=0))
    next(ag_pd)
    g = g - outer(qx * w16, qx)
    rhs_row = rhs_row - jnp.sum(qx * w16 * qz, axis=0, keepdims=True)
    eye = iota((128, 128), 0) == iota((128, 128), 1)
    rhs_col = jnp.sum(jnp.where(eye, rhs_row, 0.0), axis=1, keepdims=True)
    g = jnp.concatenate([g, jnp.broadcast_to(rhs_col, (128, 128))], axis=1)
    o = iota((128, 128), 0)
    oc, op = lax.shift_right_logical(o, 6), jnp.bitwise_and(lax.shift_right_logical(o, 4), 3)
    oq, oz = jnp.bitwise_and(lax.shift_right_logical(o, 2), 3), jnp.bitwise_and(o, 3)
    device = oc + op * (8 - 6 * oc) + oq * (2 + 6 * oc) + oz * 32
    order = (iota((128, 128), 1) == device).astype(F32).astype(BF16)
    s["g"][...] = sum(dot(order, v) for v in split3(g)).reshape(128, 1, 256)
    g_wait = cross(s["g"].at[pl.ds(theirs, 64)], s["g_cr"])
    g_wait()
    s["g_a"][...] = s["g"][pl.ds(mine, 64)] + s["g_cr"][...]
    g_wait = scatter(s["g_a"], s["g_got"])

    @pl.loop(0, 4)
    def _(g):
        rows = pl.ds(pl.multiple_of(g * 512, 512), 512)
        got = jnp.zeros((512, 256), F32)
        for k in range(8):
            got += dot(s["dy_oh"][k, rows, :], s["mh"][blk(k, 256), :])
        xt_ref[rows, :] = s["v"][rows, :] - (got[:, 0:128] + got[:, 128:256])

    def pick_z(index_row, mz):
        high = lax.shift_right_logical(index_row, 7)
        low = jnp.bitwise_and(index_row, 127)
        parts = jnp.concatenate([v.astype(F32) for v in split3(mz)], axis=0).astype(BF16)
        out = []
        for i in range(16):
            hot = (jnp.broadcast_to(low[:, blk(i)], (128, 128)) == sub).astype(F32).astype(BF16)
            got = dot(parts, hot)
            got = got[0:16] + got[16:32] + got[32:48]
            out.append(jnp.sum(jnp.where(high[:, blk(i)] == sub_id, got, 0.0), axis=0, keepdims=True))
        return jnp.concatenate(out, axis=1)

    z_row = s["z"][...] - pick_z(dy_row, mz)

    def pick_half(half):
        @pl.loop(0, 4)
        def _(g):
            rows = pl.ds(pl.multiple_of(g * 512, 512), 512)
            got = jnp.zeros((512, 256), F32)
            for j in range(4):
                part = pl.ds(pl.multiple_of(1024 * half + 256 * j, 256), 256)
                got += dot(s["pd_oh"][4 * half + j, rows, :], s["mh"][part, :])
            xt_ref[rows, :] -= got[:, 0:128] + got[:, 128:256]

    for i, (half, first) in enumerate(ag_pd):
        plane_halves("pd", half, first)
        if i in (3, 7):
            pick_half(half)

    zt_ref[...] = z_row - pick_z(po_row * 16 + pl_row, s["pd_mz"][...].reshape(16, 128))
    g_wait()
    g_row = jnp.sum(s["g_got"][...], axis=0) / total_rows
    gram_ref[...] = g_row[:, 0:128]
    rhs_ref[...] = g_row[:, 128:129]
    for wait in sends:
        wait()


def put_out(x_in, z_in, g_in, r_in, x_out, z_out, g_out, r_out, x_buf, z_buf, g_buf, r_buf, sem_in, sem_out):
    pairs = [(x_in.at[blk(i, 512)], x_buf.at[blk(i, 512)], x_out.at[blk(i, 512)]) for i in range(4)]
    pairs += [(z_in, z_buf, z_out), (g_in, g_buf, g_out), (r_in, r_buf, r_out)]
    loads = [pltpu.make_async_copy(src, buf, sem_in.at[i]) for i, (src, buf, _) in enumerate(pairs)]
    stores = [pltpu.make_async_copy(buf, dst, sem_out.at[i]) for i, (_, buf, dst) in enumerate(pairs)]
    for load in loads:
        load.start()
    for load, store in zip(loads, stores):
        load.wait()
        store.start()
    for store in stores:
        store.wait()


def scratch():
    v = pltpu.VMEM
    shapes = {
        "wc": v((R, 128), F32), "dyc": v((R, 128), F32), "pdc": v((R, 128), F32), "fc": v((R, 128), BF16),
        "ft": v((128, R), BF16), "fm": v((128, 256), BF16), "wv": v((R, 256), BF16), "v": v((R, 128), F32),
        "z": v((1, R), F32), "lh": v((512, R), BF16), "mh": v((R, 256), BF16),
        "dy_oh": v((8, R, 256), BF16), "pd_oh": v((8, R, 256), BF16), "mm": v((8, 32, 256), BF16),
        "f": v((128, 1, 128), F32), "f_cr": v((64, 1, 128), F32), "f_a": v((64, 2, 128), F32),
        "f_got": v((64, 2, 128), F32), "pd_first": v((3, 16, 17, 128), F32), "pd_b": v((16, 17, 128), F32),
        "ml": v((512, 1024), BF16), "mr": v((128, 1024), BF16), "vs": v((R, 256), BF16), "lg": v((272, R), BF16),
        "g": v((128, 1, 256), F32), "g_cr": v((64, 1, 256), F32), "g_a": v((64, 1, 256), F32),
        "g_got": v((64, 1, 256), F32),
    }
    for name, slots in (("dy", 64), ("pd", 16)):
        shapes[name + "_own"] = v((16, R), BF16)
        shapes[name + "_loc"] = v((16, R), BF16)
        shapes[name + "_ob"] = v((128, R), BF16)
        shapes[name + "_t"] = v((128, 17, 128), F32)
        shapes[name + "_cr"] = v((64, 17, 128), F32)
        shapes[name + "_a"] = v((64, 17, 128), F32)
        shapes[name + "_got"] = v((slots, 17, 128), F32)
        shapes[name + "_m"] = v((2, 64, 17, 128), F32)
        shapes[name + "_mz"] = v((8, 2, 128), F32)
    shapes["send"] = pltpu.SemaphoreType.DMA((32,))
    shapes["recv"] = pltpu.SemaphoreType.DMA((32,))
    return shapes


def shards(total_rows, covariates, outcome, predictor, firm_id, dy_id, pd_owner, pd_local):
    owner = pd_owner.reshape(R)
    rows = [v.reshape(1, R) for v in (outcome, predictor, firm_id, dy_id, owner, pd_local)]
    squares = [v.reshape(16, 128) for v in (predictor, firm_id, dy_id, owner, pd_local)]
    vmem = pl.BlockSpec(memory_space=pltpu.VMEM)
    xt, zt, gram, rhs = pl.pallas_call(
        functools.partial(kernel, total_rows),
        out_shape=(jax.ShapeDtypeStruct((R, 128), F32), jax.ShapeDtypeStruct((1, R), F32),
                   jax.ShapeDtypeStruct((1, 128), F32), jax.ShapeDtypeStruct((1, 1), F32)),
        in_specs=[vmem] * 12,
        out_specs=(vmem,) * 4,
        scratch_shapes=[scratch()],
        compiler_params=pltpu.CompilerParams(
            collective_id=0, has_side_effects=True, vmem_limit_bytes=63 * 1024 * 1024),
        name="demean",
    )(covariates, *rows, *squares)
    xt, zt, gram, rhs = pl.pallas_call(
        put_out,
        out_shape=(jax.ShapeDtypeStruct((R, 128), F32), jax.ShapeDtypeStruct((1, R), F32),
                   jax.ShapeDtypeStruct((1, 128), F32), jax.ShapeDtypeStruct((1, 1), F32)),
        in_specs=[pl.BlockSpec(memory_space=pl.ANY)] * 4,
        out_specs=[pl.BlockSpec(memory_space=pl.ANY)] * 4,
        scratch_shapes=[pltpu.VMEM(n, F32) for n in ((R, 128), (1, R), (1, 128), (1, 1))]
        + [pltpu.SemaphoreType.DMA((7,)), pltpu.SemaphoreType.DMA((7,))],
        name="put_out",
    )(xt, zt, gram, rhs)
    return xt, zt.reshape(R), gram, rhs.reshape(1)


def solution(mesh):
    specs = (P("rows", None), P("rows"), P("rows"), P("rows"), P("rows"), P("rows", None), P("rows"))
    out_specs = (P("rows", None), P("rows"), P("rows", None), P("rows"))
    return jax.shard_map(functools.partial(shards, float(R * 128)), mesh=mesh, in_specs=specs,
                         out_specs=out_specs, check_vma=False)
```
